256 devices in a mesh: row: 8 (over x, z_lo), col: 32 (over z_hi, y, core).
Axes of the slice: x: 4, y: 4, z: 8 (z_hi: 4, z_lo: 2; z = z_hi * 2 + z_lo), core: 2. Of those that a mesh axis runs over, the one named last changes fastest.
Arguments:
- layer_input: bfloat16 [40960, 3072], P(('row', 'col')), may hold values from -0.5 to 0.5
- queries: bfloat16 [40960, 128], P(('row', 'col')), may hold values from -7 to 7
- key_states: bfloat16 [40960, 128], P(('row', 'col')), may hold values from -7 to 7
- value_states: bfloat16 [40960, 128], P(('row', 'col')), may hold values from -6 to 6
- forward_out: bfloat16 [40960, 128], P(('row', 'col')), may hold values from -1.5 to 1.5
- out_grad: bfloat16 [40960, 128], P(('row', 'col')), may hold values from -12 to 12
- token_pos: int32 [40960], replicated, may hold values from 0 to 40959, as said below
- block_sample: int32 [320], replicated, may hold values from 0 to 39, never falling along the last dimension, each value on 1 to 32 neighbouring positions
Outputs:
- query_grad: bfloat16 [40960, 128], P(('row', 'col'))
- key_grad: bfloat16 [40960, 128], P(('row', 'col'))
- value_grad: bfloat16 [40960, 128], P(('row', 'col'))
- weight_grad: float32 [3072, 384], P('col')
The draws below stay inside these ranges and needn't reach their ends.
Inputs may be any that keep to these rules, and one draw needn't show every extreme that they name: `token_pos`: each packed position appears in exactly one slot. `block_sample`: never falling along the blocks; every sample spans 1 to 32 blocks and one spans exactly 32.
All inputs are finite; a program needn't handle non-finite values.
Results may differ from the reference program's by a relative error of at most 0.019.
Values may be sent and summed in bfloat16 or wider, within the bound.
A program may use at most 64 MiB of HBM per device.

```python
import math
import jax
import jax.numpy as jnp
import numpy as np
from jax import lax

D = 3072
HD = 128
TOK_DEV = 160
BLK = 128
S = 40960
TOKQ = 5120
TOKK = 1280
NBLK = 320
N_ROW = 8
N_COL = 32


def slot_positions(key):
    return jax.random.permutation(jax.random.fold_in(key, 7), S).astype(jnp.int32)


def draw_token_pos(key, part):
    return slot_positions(key)


def draw_queries(key, part):
    base_key = jax.random.fold_in(key, 21)
    values = jnp.clip(1.2 * jax.random.normal(base_key, (S, HD), jnp.float32), -7.0, 7.0)
    return values.astype(jnp.bfloat16)


def draw_key_states(key, part):
    base_key = jax.random.fold_in(key, 22)
    values = jnp.clip(1.2 * jax.random.normal(base_key, (S, HD), jnp.float32), -7.0, 7.0)
    return values.astype(jnp.bfloat16)


def with_spikes(entries, rng, source, target, blocks, factor):
    def block_of(dim):
        return (jnp.arange(entries.shape[dim]) // (entries.shape[dim] // blocks)).reshape((-1,) + (1,) * (entries.ndim - 1 - dim))

    one_side = jax.random.permutation(rng, blocks)[block_of(target)]
    other_side = (block_of(target) + blocks // 2) % blocks
    return jnp.where((block_of(source) == one_side) | (block_of(source) == other_side), factor * entries, entries)


def block_scale(stream_key, extent, pieces, low, largest):
    def one(position, shards_of):
        steps = jax.random.uniform(jax.random.fold_in(jax.random.fold_in(stream_key, 6), position), (shards_of,), jnp.float32, low / len(pieces), largest / len(pieces))
        return jnp.repeat(jnp.exp(steps), extent[position] // shards_of).reshape((-1,) + (1,) * (len(extent) - position - 1))

    level = one(*pieces[0])
    for cut in pieces[1:]:
        level = level * one(*cut)
    return level


def length_profile(number_of, total, reach, slope):
    weights = [(1 << 20) // math.isqrt(grade ** slope) + 1 for grade in range(2, number_of + 1)]
    spare, given = total - reach - (number_of - 1), [1] * (number_of - 1)
    while spare > 0:
        free = [i for i in range(number_of - 1) if given[i] < reach]
        whole, left = sum([weights[i] for i in free]), spare
        for i in free:
            more = min(reach - given[i], max(1, left * weights[i] // whole), spare)
            given[i] = given[i] + more
            spare = spare - more
    return np.array([reach] + given)


def uneven(own_key, amount, total, most, skew):
    if amount == 2:
        one = jax.random.randint(own_key, (), max(1, total - most), min(most, total - 1) + 1)
        return jnp.stack([one, total - one])
    tallies = jnp.asarray(length_profile(amount, total, most, skew), jnp.int32)
    couples = (amount - 1) // 2
    giver, taker = tallies[1:1 + 2 * couples:2], tallies[2:2 + 2 * couples:2]
    slack = jnp.minimum(giver - 1, most - taker)
    shifted = jax.random.randint(jax.random.fold_in(own_key, 1), (couples,), 0, 1 << 20) % (slack + 1)
    tallies = tallies.at[1:1 + 2 * couples:2].set(giver - shifted).at[2:2 + 2 * couples:2].set(taker + shifted)
    return tallies[jax.random.permutation(jax.random.fold_in(own_key, 2), amount)]


def centred(stream_key, shape, scale, bound, cuts=(), kind=jnp.bfloat16):
    drawn = jax.random.normal(stream_key, shape, jnp.float32) * scale
    if len(cuts) > 0:
        drawn = block_scale(stream_key, shape, cuts, -0.22, 0.18) * drawn
    return jnp.clip(drawn, min=-bound, max=bound).astype(kind)


def heavy_noise(key, extent, spread, limit, cuts, heavy, kind=jnp.bfloat16):
    values = spread * jax.random.normal(key, extent, jnp.float32)
    if cuts:
        values = values * block_scale(key, extent, cuts, -0.22, 0.18)
    return jnp.clip(with_spikes(values, jax.random.fold_in(key, 3), *heavy), -limit, limit).astype(kind)


def setup_inputs(seed: int = 0) -> dict:
    arg_keys = jax.random.split(jax.random.key(seed), 9)
    return {
        "layer_input": heavy_noise(arg_keys[0], (S, D), 0.02, 0.5, ((0, 256),), (0, 1, 256, 6.0)),
        "queries": draw_queries(jax.random.fold_in(arg_keys[8], 71), 0),
        "key_states": draw_key_states(jax.random.fold_in(arg_keys[8], 71), 0),
        "value_states": centred(arg_keys[3], (S, HD), 1.0, 6.0, ((0, 256),)),
        "forward_out": centred(arg_keys[4], (S, HD), 0.25, 1.5, ((0, 256),)),
        "out_grad": centred(arg_keys[5], (S, HD), 2.0, 12.0, ((0, 256),)),
        "token_pos": draw_token_pos(jax.random.fold_in(arg_keys[8], 71), 0),
        "block_sample": jnp.searchsorted(jnp.cumsum(uneven(arg_keys[7], NBLK // 8, NBLK, min(32, NBLK // 2), 2)), jnp.arange(NBLK), side="right").astype(jnp.int32),
    }


NEG_FILL = -1e30


def rounded(values):
    return lax.optimization_barrier(values.astype(jnp.bfloat16)).astype(jnp.float32)


def reference(layer_input, queries, key_states, value_states, forward_out, out_grad, token_pos, block_sample):
    score_scale = 1.0 / (HD ** 0.5)
    sample_ids = jnp.take(block_sample, (token_pos // BLK).astype(jnp.int32))
    row_delta = jnp.sum(out_grad.astype(jnp.float32) * forward_out.astype(jnp.float32), axis=1)

    def by_row(array):
        return array.reshape((N_ROW, TOKQ) + array.shape[1:])

    def by_col(array):
        grouped = array.reshape((N_ROW, N_COL, TOK_DEV) + array.shape[1:])
        return jnp.swapaxes(grouped, 0, 1).reshape((N_COL, TOKK) + array.shape[1:])

    col_keys = by_col(key_states)
    col_values = by_col(value_states)
    col_samples = by_col(sample_ids)

    def row_step(running, row_inputs):
        key_acc, value_acc = running
        query_rows, grad_rows, delta_rows, query_samples = row_inputs

        def masked(key_rows, key_samples):
            scores = jnp.dot(query_rows, key_rows.T, preferred_element_type=jnp.float32) * score_scale
            live_pairs = query_samples[:, None] == key_samples[None, :]
            return jnp.where(live_pairs, scores, NEG_FILL), live_pairs

        def stat_step(stats, col_inputs):
            old_peak, row_sum = stats
            scores, live_pairs = masked(col_inputs[0], col_inputs[1])
            new_peak = jnp.maximum(old_peak, jnp.max(scores, axis=1))
            fresh = jnp.sum(jnp.where(live_pairs, jnp.exp(scores - new_peak[:, None]), 0.0), axis=1)
            return (new_peak, row_sum * jnp.exp(old_peak - new_peak) + fresh), None

        start_stats = (jnp.full((TOKQ,), NEG_FILL, jnp.float32), jnp.zeros((TOKQ,), jnp.float32))
        (row_peak, row_total), unused = lax.scan(stat_step, start_stats, (col_keys, col_samples))

        def grad_step(query_acc, col_inputs):
            key_rows, value_rows, key_samples = col_inputs
            scores, live_pairs = masked(key_rows, key_samples)
            prob_rows = jnp.where(live_pairs, jnp.exp(scores - row_peak[:, None]), 0.0) / row_total[:, None]
            prob_low = prob_rows.astype(jnp.bfloat16)
            value_part = jnp.dot(prob_low.T, grad_rows, preferred_element_type=jnp.float32)
            prob_grad = jnp.dot(grad_rows, value_rows.T, preferred_element_type=jnp.float32)
            score_grad = (prob_rows * (prob_grad - delta_rows[:, None])).astype(jnp.bfloat16)
            query_part = jnp.dot(score_grad, key_rows, preferred_element_type=jnp.float32) * score_scale
            key_part = jnp.dot(score_grad.T, query_rows, preferred_element_type=jnp.float32) * score_scale
            return query_acc + rounded(query_part), (rounded(key_part), rounded(value_part))

        query_acc, (key_parts, value_parts) = lax.scan(
            grad_step, jnp.zeros((TOKQ, HD), jnp.float32), (col_keys, col_values, col_samples))
        return (key_acc + key_parts, value_acc + value_parts), query_acc.astype(jnp.bfloat16)

    zero_acc = jnp.zeros((N_COL, TOKK, HD), jnp.float32)
    (key_acc, value_acc), query_grad = lax.scan(
        row_step, (zero_acc, zero_acc),
        (by_row(queries), by_row(out_grad), by_row(row_delta), by_row(sample_ids)))
    query_grad = query_grad.reshape(S, HD)

    def unpack(acc):
        return jnp.swapaxes(acc.reshape(N_COL, N_ROW, TOK_DEV, HD), 0, 1).reshape(S, HD).astype(jnp.bfloat16)

    key_grad = unpack(key_acc)
    value_grad = unpack(value_acc)
    all_grads = jnp.concatenate([query_grad, key_grad, value_grad], axis=1)
    weight_grad = jnp.dot(layer_input.T, all_grads, preferred_element_type=jnp.float32)
    return query_grad, key_grad, value_grad, weight_grad
```

```python
import math

import jax
import jax.numpy as jnp
from jax import lax
from jax.experimental import pallas as pl
from jax.experimental.pallas import tpu as pltpu
from jax.sharding import Mesh
from jax.sharding import PartitionSpec as P

BLK = 128
BIG = 16384.0
MESH = pl.DeviceIdType.MESH
NT = (((1,), (1,)), ((), ()))
AXES = ("x", "zl", "zh", "y", "c")
bf16 = jnp.bfloat16
f32 = jnp.float32


def dot_nt(a, b, **kw):
    return lax.dot_general(a, b, NT, preferred_element_type=f32, **kw)


def dot(a, b):
    return jnp.dot(a, b, preferred_element_type=f32)


def as_column(row):
    return jnp.transpose(jnp.broadcast_to(row, (128, row.shape[1])))


def eye(n):
    return (
        lax.broadcasted_iota(jnp.int32, (n, n), 0) == lax.broadcasted_iota(jnp.int32, (n, n), 1)
    ).astype(bf16)


class Group:
    def __init__(self, size, me, device_of, send, recv):
        self.size, self.me, self.device_of, self.send, self.recv = size, me, device_of, send, recv

    def copy(self, k, member, src, dst):
        return pltpu.make_async_remote_copy(
            src_ref=src,
            dst_ref=dst,
            send_sem=self.send.at[k, member],
            recv_sem=self.recv.at[k, self.me],
            device_id=self.device_of(member),
            device_id_type=MESH,
        )

    def landed(self, k, member, src, dst):
        return pltpu.make_async_remote_copy(
            src_ref=src,
            dst_ref=dst,
            send_sem=self.send.at[k, member],
            recv_sem=self.recv.at[k, member],
            device_id=self.device_of(member),
            device_id_type=MESH,
        )

    def others(self, body):
        def step(i, carry):
            body(lax.rem(self.me + i, self.size))
            return carry

        lax.fori_loop(1, self.size, step, 0)


def kernel(
    dims, q_in, k_in, v_in, o_in, g_in, x_in, pos_ref, span_ref,
    dq_out, dk_out, dv_out, wg_out,
    qb, gb, db, kb, vb, fq, fk, kt, et, ut, s_scr, dqt, st, rr, gs, qs,
    dqs, dqr, kvs, kvr, xt, xr, gr, ws, wr, ar,
    q_send, q_recv, k_send, k_recv, p_send, p_recv, w_send, w_recv, a_send, a_recv, own_sem,
):
    nx, nzl, nzh, ny, nc = dims
    tok = q_in.shape[0]
    chunk = wg_out.shape[0]
    x, zl, zh, y, c = (lax.axis_index(a) for a in AXES)
    nq, nk, npc, nr = nzh * nzl * nc, nx * ny, ny * nc, nx * nzl
    me_q = (zh * nzl + zl) * nc + c
    me_k = x * ny + y
    me_p = y * nc + c
    me_r = x * nzl + zl
    n_query, n_key = nq * tok, nk * tok

    def rows_of(s):
        return pl.ds(pl.multiple_of(s * tok, tok), tok)

    def dev(ax, azl, azh, ay, ac):
        return (ax, azl, azh, ay, ac)

    def q_dev(s):
        z = s // nc
        return dev(x, z % nzl, z // nzl, y, s % nc)

    def k_dev(s):
        return dev(s // ny, zl, zh, s % ny, c)

    def p_dev(s):
        return dev(x, zl, zh, s // nc, s % nc)

    def w_dev(s):
        return dev(x, zl, s, y, c)

    def a_dev(s):
        return dev(s // nzl, s % nzl, zh, y, c)

    gq = Group(nq, me_q, q_dev, q_send, q_recv)
    gk = Group(nk, me_k, k_dev, k_send, k_recv)
    gp = Group(npc, me_p, p_dev, p_send, p_recv)
    gw = Group(nzh, zh, w_dev, w_send, w_recv)
    ga = Group(nr, me_r, a_dev, a_send, a_recv)

    barrier = pltpu.get_barrier_semaphore()
    for group in (gq, gk, gp, gw, ga):
        group.others(
            lambda s, group=group: pl.semaphore_signal(
                barrier, inc=1, device_id=group.device_of(s), device_id_type=MESH
            )
        )

    qb[rows_of(me_q), :] = q_in[...]
    gb[rows_of(me_q), :] = g_in[...]
    kb[rows_of(me_k), :] = k_in[...]
    vb[rows_of(me_k), :] = v_in[...]
    product = g_in[...].astype(f32) * o_in[...].astype(f32)
    delta = dot_nt(jnp.ones((8, product.shape[1]), f32), product, precision=lax.Precision.HIGHEST)
    db[me_q, :, 0:tok] = delta[0:1, :]
    pl.semaphore_wait(barrier, nq + nk + npc + nzh + nr - 5)

    def start_q(s):
        gq.copy(0, s, qb.at[rows_of(me_q), :], qb.at[rows_of(me_q), :]).start()
        gq.copy(1, s, gb.at[rows_of(me_q), :], gb.at[rows_of(me_q), :]).start()
        gq.copy(2, s, db.at[me_q], db.at[me_q]).start()

    def start_k(s):
        gk.copy(0, s, kb.at[rows_of(me_k), :], kb.at[rows_of(me_k), :]).start()
        gk.copy(1, s, vb.at[rows_of(me_k), :], vb.at[rows_of(me_k), :]).start()

    gk.others(start_k)
    gq.others(start_q)

    low, high = span_ref[0:1, :], span_ref[1:2, :]
    last = lax.broadcasted_iota(jnp.int32, (tok, 128), 1) == 127

    def one_hot(device, hit, always):
        index = device[0]
        for n, i in zip(dims[1:], device[1:]):
            index = index * n + i
        col = as_column(pos_ref[pl.ds(index, 1), :])[0:tok, :]
        inside = jnp.where((col >= low) & (col < high), hit, 0.0)
        return jnp.where(last, always, inside).astype(bf16)

    def query_hot(s, carry):
        fq[pl.ds(pl.multiple_of(s * tok, tok), tok), :] = one_hot(q_dev(s), BIG, -BIG)
        return carry

    def key_hot(s, carry):
        fk[pl.ds(pl.multiple_of(s * tok, tok), tok), :] = one_hot(k_dev(s), 1.0, 1.0)
        return carry

    lax.fori_loop(0, nq, query_hot, 0)
    lax.fori_loop(0, nk, key_hot, 0)

    xt[:, :, :, tok:] = jnp.zeros((npc, nzh, chunk, 256 - tok), bf16)
    gr[:, tok:, :] = jnp.zeros((npc, 256 - tok, 384), bf16)
    four = eye(4 * chunk)
    for g in range(nzh * npc // 4):
        turned = dot_nt(four, x_in[:, g * 4 * chunk : (g + 1) * 4 * chunk]).astype(bf16)
        for j in range(4):
            n = 4 * g + j
            xt[n % npc, n // npc, :, 0:tok] = turned[j * chunk : (j + 1) * chunk, :]

    def landed_k(s):
        gk.landed(0, s, kb.at[rows_of(me_k), :], kb.at[rows_of(s), :]).wait_recv()
        gk.landed(1, s, vb.at[rows_of(me_k), :], vb.at[rows_of(s), :]).wait_recv()

    def landed_q(s):
        gq.landed(0, s, qb.at[rows_of(me_q), :], qb.at[rows_of(s), :]).wait_recv()
        gq.landed(1, s, gb.at[rows_of(me_q), :], gb.at[rows_of(s), :]).wait_recv()
        gq.landed(2, s, db.at[me_q], db.at[s]).wait_recv()

    gk.others(landed_k)
    gq.others(landed_q)

    own = pltpu.make_async_copy(xt.at[me_p], xr.at[me_p], own_sem)
    own.start()
    gp.others(lambda s: gp.copy(0, s, xt.at[s], xr.at[me_p]).start())

    tq = 256
    tk = 256 if n_key % 256 == 0 else tok
    score_scale = 1.0 / math.sqrt(128.0)
    rate = score_scale / math.log(2.0)
    unit = eye(128)
    kt[...] = dot_nt(unit, kb[...]).astype(bf16)
    rr[2:3, :] = jnp.concatenate([db[s, :, 0:tok] for s in range(nq)], axis=1)

    @pl.loop(0, n_query // tq)
    def _(t):
        at = pl.ds(pl.multiple_of(t * tq, tq), tq)
        query_tile = jnp.concatenate([qb[at, :], fq[at, :]], axis=1)
        grad_tile = gb[at, :]
        top = jnp.full((8, tq), -3.0e38, f32)
        for n in range(n_key // tk):
            span = slice(n * tk, (n + 1) * tk)
            s = dot_nt(jnp.concatenate([kb[span, :], fk[span, :]], axis=1), query_tile)
            s_scr[span, :] = s
            top = jnp.maximum(top, jnp.max(s.reshape(tk // 8, 8, tq), axis=0))
        peak = jnp.max(top, axis=0, keepdims=True)
        delta_row = rr[2:3, at]
        total = jnp.zeros((8, tq), f32)
        acc = jnp.zeros((128, tq), f32)
        for n in range(n_key // tk):
            span = slice(n * tk, (n + 1) * tk)
            e = jnp.exp2((s_scr[span, :] - peak) * rate)
            total = total + jnp.sum(e.reshape(tk // 8, 8, tq), axis=0)
            u = (e * (dot_nt(vb[span, :], grad_tile) - delta_row)).astype(bf16)
            et[span, at] = e.astype(bf16)
            ut[span, at] = u
            acc = acc + dot(kt[:, span], u)
        dqt[:, at] = acc
        rr[0:1, at] = peak
        rr[1:2, at] = jnp.sum(total, axis=0, keepdims=True)

    st[me_q] = rr[0:2, :]
    gq.others(lambda s: gq.copy(3, s, st.at[me_q], st.at[me_q]).start())
    gq.others(lambda s: gq.landed(3, s, st.at[me_q], st.at[s]).wait_recv())

    peak = st[0, 0:1, :]
    for s in range(1, nq):
        peak = jnp.maximum(peak, st[s, 0:1, :])
    total = jnp.zeros_like(peak)
    for s in range(nq):
        total = total + st[s, 1:2, :] * jnp.exp2((st[s, 0:1, :] - peak) * rate)
    rr[3:4, :] = jnp.exp2((rr[0:1, :] - peak) * rate) / total

    @pl.loop(0, n_query // tq)
    def _(t):
        at = pl.ds(pl.multiple_of(t * tq, tq), tq)
        factor = rr[3:4, at]
        dqs[at, :] = jnp.transpose(dqt[:, at] * (factor * score_scale)).astype(bf16)
        col = as_column(factor)
        gs[at, :] = (gb[at, :].astype(f32) * col).astype(bf16)
        qs[at, :] = (qb[at, :].astype(f32) * (col * score_scale)).astype(bf16)

    gq.others(lambda s: gq.copy(4, s, dqs.at[rows_of(s), :], dqr.at[me_q]).start())
    dqr[me_q] = dqs[rows_of(me_q), :]

    tb = 4 * tok if n_key % (4 * tok) == 0 else tok

    @pl.loop(0, n_key // tb)
    def _(t):
        at = pl.ds(pl.multiple_of(t * tb, tb), tb)
        kvs[at, 0:128] = dot(ut[at, :], qs[...]).astype(bf16)
        kvs[at, 128:256] = dot(et[at, :], gs[...]).astype(bf16)

    gk.others(lambda s: gk.copy(2, s, kvs.at[rows_of(s), :], kvr.at[me_k]).start())
    kvr[me_k] = kvs[rows_of(me_k), :]

    gq.others(lambda s: gq.landed(4, s, dqs.at[rows_of(s), :], dqr.at[s]).wait_recv())
    acc = dqr[0].astype(f32)
    for s in range(1, nq):
        acc = acc + dqr[s].astype(f32)
    dq_out[...] = acc.astype(bf16)
    gr[me_p, 0:tok, 0:128] = acc.astype(bf16)

    def part(n, a, b, s):
        return gp.copy(n, s, gr.at[me_p, 0:tok, a:b], gr.at[me_p, 0:tok, a:b])

    def part_landed(n, a, b, s):
        gp.landed(n, s, gr.at[me_p, 0:tok, a:b], gr.at[s, 0:tok, a:b]).wait_recv()

    gp.others(lambda s: part(1, 0, 128, s).start())

    gk.others(lambda s: gk.landed(2, s, kvs.at[rows_of(s), :], kvr.at[s]).wait_recv())
    acc = kvr[0].astype(f32)
    for s in range(1, nk):
        acc = acc + kvr[s].astype(f32)
    dk_out[...] = acc[:, 0:128].astype(bf16)
    dv_out[...] = acc[:, 128:256].astype(bf16)
    gr[me_p, 0:tok, 128:384] = acc.astype(bf16)
    gp.others(lambda s: part(2, 128, 384, s).start())

    own.wait()
    gp.others(lambda s: gp.landed(0, s, xt.at[s], xr.at[s]).wait_recv())
    gp.others(lambda s: part_landed(1, 0, 128, s))
    gp.others(lambda s: part_landed(2, 128, 384, s))

    def weight_rows(n):
        acc = dot(xr[0, n], gr[0])
        for p in range(1, npc):
            acc = acc + dot(xr[p, n], gr[p])
        return acc.astype(bf16)

    def weight_step(i, carry):
        n = lax.rem(zh + i, nzh)
        ws[n] = weight_rows(n)
        gw.copy(0, n, ws.at[n], wr.at[zh]).start()
        return carry

    lax.fori_loop(1, nzh, weight_step, 0)
    wr[zh] = weight_rows(zh)
    gw.others(lambda s: gw.landed(0, s, ws.at[s], wr.at[s]).wait_recv())
    acc = wr[0].astype(f32)
    for s in range(1, nzh):
        acc = acc + wr[s].astype(f32)
    ar[me_r] = acc.astype(bf16)
    ga.others(lambda s: ga.copy(0, s, ar.at[me_r], ar.at[me_r]).start())
    ga.others(lambda s: ga.landed(0, s, ar.at[me_r], ar.at[s]).wait_recv())
    acc = ar[0].astype(f32)
    for s in range(1, nr):
        acc = acc + ar[s].astype(f32)
    wg_out[...] = acc

    def sent_q(s):
        gq.copy(0, s, qb.at[rows_of(me_q), :], qb.at[rows_of(me_q), :]).wait_send()
        gq.copy(1, s, gb.at[rows_of(me_q), :], gb.at[rows_of(me_q), :]).wait_send()
        gq.copy(2, s, db.at[me_q], db.at[me_q]).wait_send()
        gq.copy(3, s, st.at[me_q], st.at[me_q]).wait_send()
        gq.copy(4, s, dqs.at[rows_of(s), :], dqr.at[me_q]).wait_send()

    def sent_k(s):
        gk.copy(0, s, kb.at[rows_of(me_k), :], kb.at[rows_of(me_k), :]).wait_send()
        gk.copy(1, s, vb.at[rows_of(me_k), :], vb.at[rows_of(me_k), :]).wait_send()
        gk.copy(2, s, kvs.at[rows_of(s), :], kvr.at[me_k]).wait_send()

    def sent_p(s):
        gp.copy(0, s, xt.at[s], xr.at[me_p]).wait_send()
        part(1, 0, 128, s).wait_send()
        part(2, 128, 384, s).wait_send()

    gq.others(sent_q)
    gk.others(sent_k)
    gp.others(sent_p)
    gw.others(lambda s: gw.copy(0, s, ws.at[s], wr.at[zh]).wait_send())
    ga.others(lambda s: ga.copy(0, s, ar.at[me_r], ar.at[me_r]).wait_send())


def local(
    dims, layer_input, queries, key_states, value_states, forward_out, out_grad, token_pos,
    block_sample,
):
    nx, nzl, nzh, ny, nc = dims
    tok, width = queries.shape
    depth = layer_input.shape[1]
    chunk = depth // (nzh * ny * nc)
    nq, nk, npc, nr = nzh * nzl * nc, nx * ny, ny * nc, nx * nzl
    n_query, n_key = nq * tok, nk * tok
    pos = token_pos.astype(f32).reshape(-1, tok)
    pos = jnp.pad(pos, ((0, 0), (0, 256 - tok)))
    ids = jnp.arange(128, dtype=jnp.int32)
    low = BLK * jnp.sum(block_sample[None, :] < ids[:, None], axis=1)
    high = BLK * jnp.sum(block_sample[None, :] <= ids[:, None], axis=1)
    span = jnp.stack([low, high]).astype(f32)
    span = jnp.pad(span, ((0, 6), (0, 0)))
    V = pltpu.VMEM
    dma = pltpu.SemaphoreType.DMA
    scratch = [
        V((n_query, 128), bf16), V((n_query, 128), bf16), V((nq, 1, 256), f32),
        V((n_key, 128), bf16), V((n_key, 128), bf16),
        V((n_query, 128), bf16), V((n_key, 128), bf16), V((128, n_key), bf16),
        V((n_key, n_query), bf16), V((n_key, n_query), bf16), V((n_key, 256), f32),
        V((128, n_query), f32), V((nq, 2, n_query), f32), V((8, n_query), f32),
        V((n_query, 128), bf16), V((n_query, 128), bf16),
        V((n_query, 128), bf16), V((nq, tok, 128), bf16),
        V((n_key, 256), bf16), V((nk, tok, 256), bf16),
        V((npc, nzh, chunk, 256), bf16), V((npc, nzh, chunk, 256), bf16),
        V((npc, 256, 384), bf16), V((nzh, chunk, 384), bf16), V((nzh, chunk, 384), bf16),
        V((nr, chunk, 384), bf16),
        dma((5, nq)), dma((5, nq)), dma((3, nk)), dma((3, nk)), dma((3, npc)), dma((3, npc)),
        dma((1, nzh)), dma((1, nzh)), dma((1, nr)), dma((1, nr)), dma,
    ]

    def body(*refs):
        kernel(dims, *refs)

    vmem = pl.BlockSpec(memory_space=pltpu.VMEM)
    grad = jax.ShapeDtypeStruct((tok, 128), bf16)
    return pl.pallas_call(
        body,
        out_shape=(grad, grad, grad, jax.ShapeDtypeStruct((chunk, 384), f32)),
        in_specs=[vmem] * 8,
        out_specs=(vmem,) * 4,
        scratch_shapes=scratch,
        compiler_params=pltpu.CompilerParams(
            collective_id=0, has_side_effects=True, vmem_limit_bytes=64 * 2**20
        ),
        name="packed_backward",
    )(queries, key_states, value_states, forward_out, out_grad, layer_input, pos, span)


def on_mesh(finer):
    dims = tuple(finer.shape[a] for a in AXES)
    slots, cols = P(AXES, None), P(("zh", "y", "c"), None)
    return jax.shard_map(
        lambda *args: local(dims, *args),
        mesh=finer,
        in_specs=(slots,) * 6 + (P(), P()),
        out_specs=(slots, slots, slots, cols),
        check_vma=False,
    )


def solution(mesh):
    return on_mesh(Mesh(mesh.devices.reshape(4, 2, 4, 4, 2), AXES))
```

```python
import math

import jax
import jax.numpy as jnp
from jax import lax
from jax.experimental import pallas as pl
from jax.experimental.pallas import tpu as pltpu
from jax.sharding import Mesh
from jax.sharding import PartitionSpec as P

BLK = 128
BIG = 16384.0
MESH = pl.DeviceIdType.MESH
NT = (((1,), (1,)), ((), ()))
AXES = ("x", "zl", "zh", "y", "c")
bf16 = jnp.bfloat16
f32 = jnp.float32


def dot_nt(a, b, **kw):
    return lax.dot_general(a, b, NT, preferred_element_type=f32, **kw)


def dot(a, b):
    return jnp.dot(a, b, preferred_element_type=f32)


def as_column(row):
    return jnp.transpose(jnp.broadcast_to(row, (128, row.shape[1])))


def eye(n):
    return (
        lax.broadcasted_iota(jnp.int32, (n, n), 0) == lax.broadcasted_iota(jnp.int32, (n, n), 1)
    ).astype(bf16)


def as_row(col):
    return jnp.transpose(jnp.broadcast_to(col, (col.shape[0], 128)))[0:1, :]


def by_distance(n):
    return sorted(range(1, n), key=lambda d: -min(d, n - d))


def kernel(
    dims, q_in, k_in, v_in, o_in, g_in, x_in, pos_ref, block_ref,
    dq_out, dk_out, dv_out, wg_out,
    qg, db, kv, fq, fk, kt, et, ut, s_scr, dqt, st, rr, gs, qs, dk_acc, dv_acc,
    dqs, dqr, dks, dvs, dkr, dvr, xt, xr, gr, ws, wr, ar,
    q_send, q_recv, f_send, t_send, t_recv, k_send, k_recv, x_send, x_recv, p_send, h_send, p_recv,
    w_send, w_recv, a_send, a_recv, own_sem,
):
    nx, nzl, nzh, ny, nc = dims
    tok = q_in.shape[0]
    chunk = wg_out.shape[0]
    x, zl, zh, y, c = (lax.axis_index(a) for a in AXES)
    nz = nzh * nzl
    nq, nk, npc, nr = nz * nc, nx * ny, ny * nc, nx * nzl
    z = zh * nzl + zl
    me_q = z * nc + c
    me_k = x * ny + y
    me_p = y * nc + c
    me_r = x * nzl + zl
    n_query, n_key = nq * tok, nk * tok
    half = n_query // 2

    def rows_of(s):
        return pl.ds(pl.multiple_of(s * tok, tok), tok)

    def at_z(w, core):
        return (x, lax.rem(w, nzl), w // nzl, y, core)

    def at_xy(a, b):
        return (a, zl, zh, b, c)

    def at_p(s):
        return (x, zl, zh, s // nc, lax.rem(s, nc))

    def at_zh(s):
        return (x, zl, s, y, c)

    def at_r(s):
        return (s // nzl, lax.rem(s, nzl), zh, y, c)

    other = 1 - c
    partner = (x, zl, zh, y, other)

    def send(src, dst, send_sem, recv_sem, device):
        return pltpu.make_async_remote_copy(
            src_ref=src, dst_ref=dst, send_sem=send_sem, recv_sem=recv_sem,
            device_id=device, device_id_type=MESH,
        )

    def each(me, size, body):
        def step(i, carry):
            body(lax.rem(me + i, size))
            return carry

        lax.fori_loop(1, size, step, 0)

    def each_z(body):
        for d in by_distance(nz):
            body(lax.rem(z + d, nz))

    def each_y(body):
        for d in by_distance(ny):
            body(lax.rem(y + d, ny))

    def each_xy(body):
        pairs = [(a, b) for a in range(nx) for b in range(ny) if a or b]
        for a, b in sorted(pairs, key=lambda p: -min(p[0], nx - p[0]) - min(p[1], ny - p[1])):
            body(lax.rem(x + a, nx), lax.rem(y + b, ny))

    barrier = pltpu.get_barrier_semaphore()

    def hello(device):
        pl.semaphore_signal(barrier, inc=1, device_id=device, device_id_type=MESH)

    each(me_q, nq, lambda s: hello(at_z(s // nc, lax.rem(s, nc))))
    each(me_k, nk, lambda s: hello(at_xy(s // ny, lax.rem(s, ny))))
    each(me_p, npc, lambda s: hello(at_p(s)))
    each(zh, nzh, lambda s: hello(at_zh(s)))
    each(me_r, nr, lambda s: hello(at_r(s)))

    mine_q, mine_k = rows_of(me_q), rows_of(me_k)
    qg[mine_q, 0:128] = q_in[...]
    qg[mine_q, 128:256] = g_in[...]
    kv[mine_k, 0:128] = k_in[...]
    kv[mine_k, 128:256] = v_in[...]
    product = g_in[...].astype(f32) * o_in[...].astype(f32)
    delta = dot_nt(jnp.ones((8, product.shape[1]), f32), product, precision=lax.Precision.HIGHEST)
    db[me_q, :, 0:tok] = delta[0:1, :]
    pl.semaphore_wait(barrier, nq + nk + npc + nzh + nr - 5)

    def q_block(s, device, sem, n):
        rows = rows_of(s)
        return (
            send(qg.at[rows, :], qg.at[rows, :], sem.at[0, n], q_recv.at[0, s], device),
            send(db.at[s], db.at[s], sem.at[1, n], q_recv.at[1, s], device),
        )

    def k_block(s, device, n):
        rows = rows_of(s)
        return send(kv.at[rows, :], kv.at[rows, :], k_send.at[0, n], k_recv.at[0, s], device)

    def start_q(s, device, sem, n):
        for copy in q_block(s, device, sem, n):
            copy.start()

    each_z(lambda w: start_q(me_q, at_z(w, c), q_send, w))
    each_xy(lambda a, b: k_block(me_k, at_xy(a, b), a * ny + b).start())
    start_q(me_q, partner, f_send, z)

    samples = lax.broadcasted_iota(jnp.int32, (128, block_ref.shape[1]), 0)
    below = jnp.where(block_ref[...] < samples, 1.0, 0.0)
    upto = jnp.where(block_ref[...] <= samples, 1.0, 0.0)
    low = as_row(jnp.sum(below, axis=1, keepdims=True) * float(BLK))
    high = as_row(jnp.sum(upto, axis=1, keepdims=True) * float(BLK))
    last = lax.broadcasted_iota(jnp.int32, (tok, 128), 1) == 127
    rest = jnp.zeros((1, 256 - tok), f32)

    def one_hot(device, hit, always):
        index = device[0]
        for n, i in zip(dims[1:], device[1:]):
            index = index * n + i
        row = jnp.concatenate([pos_ref[pl.ds(index, 1), :].astype(f32), rest], axis=1)
        col = as_column(row)[0:tok, :]
        inside = jnp.where((col >= low) & (col < high), hit, 0.0)
        return jnp.where(last, always, inside).astype(bf16)

    def query_hot(s, carry):
        fq[rows_of(s), :] = one_hot(at_z(s // nc, lax.rem(s, nc)), BIG, -BIG)
        return carry

    def key_hot(s, carry):
        fk[rows_of(s), :] = one_hot(at_xy(s // ny, lax.rem(s, ny)), 1.0, 1.0)
        return carry

    lax.fori_loop(0, nk, key_hot, 0)

    def land_q(w):
        s = w * nc + c
        for copy in q_block(s, partner, f_send, w):
            copy.wait_recv()
        start_q(s, partner, f_send, w)

    each_z(land_q)
    lax.fori_loop(0, nq, query_hot, 0)

    xt[:, :, tok:] = jnp.zeros((npc, nzh * chunk, 256 - tok), bf16)
    gr[:, tok:, :] = jnp.zeros((npc, 256 - tok, 384), bf16)
    four = eye(4 * chunk)
    for g in range(nzh * npc // 4):
        turned = dot_nt(four, x_in[:, g * 4 * chunk : (g + 1) * 4 * chunk]).astype(bf16)
        for j in range(4):
            n = 4 * g + j
            rows = slice(n // npc * chunk, (n // npc + 1) * chunk)
            xt[n % npc, rows, 0:tok] = turned[j * chunk : (j + 1) * chunk, :]

    each_xy(lambda a, b: k_block(a * ny + b, at_xy(a, b), a * ny + b).wait_recv())

    def land_other(w, carry):
        for copy in q_block(w * nc + other, partner, f_send, w):
            copy.wait_recv()
        return carry

    lax.fori_loop(0, nz, land_other, 0)

    def x_block(s, n):
        return send(xt.at[s], xr.at[n], x_send.at[s], x_recv.at[n], at_p(s))

    own = pltpu.make_async_copy(xt.at[me_p], xr.at[me_p], own_sem)
    own.start()
    each(me_p, npc, lambda s: x_block(s, me_p).start())

    tq = 256 if half % 256 == 0 else 128
    tk = 256 if n_key % 256 == 0 else tok
    score_scale = 1.0 / math.sqrt(128.0)
    rate = score_scale / math.log(2.0)
    kt[...] = dot_nt(eye(128), kv[:, 0:128]).astype(bf16)
    rr[2:3, :] = jnp.concatenate([db[s, :, 0:tok] for s in range(nq)], axis=1)

    def score_tile(t, with_dq):
        at = pl.ds(pl.multiple_of(t * tq, tq), tq)
        query_tile = jnp.concatenate([qg[at, 0:128], fq[at, :]], axis=1)
        grad_tile = qg[at, 128:256]
        top = jnp.full((8, tq), -3.0e38, f32)
        for n in range(n_key // tk):
            span = slice(n * tk, (n + 1) * tk)
            s = dot_nt(jnp.concatenate([kv[span, 0:128], fk[span, :]], axis=1), query_tile)
            s_scr[span, 0:tq] = s
            top = jnp.maximum(top, jnp.max(s.reshape(tk // 8, 8, tq), axis=0))
        peak = jnp.max(top, axis=0, keepdims=True)
        delta_row = rr[2:3, at]
        total = jnp.zeros((8, tq), f32)
        acc = jnp.zeros((128, tq), f32)
        for n in range(n_key // tk):
            span = slice(n * tk, (n + 1) * tk)
            e = jnp.exp2((s_scr[span, 0:tq] - peak) * rate)
            total = total + jnp.sum(e.reshape(tk // 8, 8, tq), axis=0)
            u = (e * (dot_nt(kv[span, 128:256], grad_tile) - delta_row)).astype(bf16)
            et[span, at] = e.astype(bf16)
            ut[span, at] = u
            if with_dq:
                acc = acc + dot(kt[:, span], u)
        if with_dq:
            dqt[:, at] = acc
        rr[0:1, at] = peak
        rr[1:2, at] = jnp.sum(total, axis=0, keepdims=True)

    def st_block(h, s, device, n):
        return send(st.at[h, s], st.at[h, s], t_send.at[h, n], t_recv.at[h, s], device)

    def send_stats(h):
        st[h, me_q] = rr[0:2, h * half : (h + 1) * half]
        each(me_q, nq, lambda s: st_block(h, me_q, at_z(s // nc, lax.rem(s, nc)), s).start())

    def dq_block(s, n):
        device = at_z(s // nc, lax.rem(s, nc))
        return send(dqs.at[rows_of(s), :], dqr.at[n], q_send.at[2, s], q_recv.at[2, n], device)

    def factors(h):
        each(me_q, nq, lambda s: st_block(h, s, partner, s).wait_recv())
        part = slice(h * half, (h + 1) * half)
        peak = st[h, 0, 0:1, :]
        for s in range(1, nq):
            peak = jnp.maximum(peak, st[h, s, 0:1, :])
        total = jnp.zeros_like(peak)
        for s in range(nq):
            total = total + st[h, s, 1:2, :] * jnp.exp2((st[h, s, 0:1, :] - peak) * rate)
        rr[3:4, part] = jnp.exp2((rr[0:1, part] - peak) * rate) / total

        @pl.loop(h * half // tq, (h + 1) * half // tq)
        def _(t):
            at = pl.ds(pl.multiple_of(t * tq, tq), tq)
            factor = rr[3:4, at]
            dqs[at, :] = jnp.transpose(dqt[:, at] * (factor * score_scale)).astype(bf16)
            col = as_column(factor)
            gs[at, :] = (qg[at, 128:256].astype(f32) * col).astype(bf16)
            qs[at, :] = (qg[at, 0:128].astype(f32) * (col * score_scale)).astype(bf16)

        def send_dq(s, carry):
            @pl.when(s != me_q)
            def _():
                dq_block(s, me_q).start()

            return carry

        lax.fori_loop(h * nq // 2, (h + 1) * nq // 2, send_dq, 0)

    @pl.loop(0, half // tq)
    def _(t):
        score_tile(t, True)

    send_stats(0)

    @pl.loop(half // tq, n_query // tq)
    def _(t):
        score_tile(t, False)

    send_stats(1)

    @pl.loop(half // tq, n_query // tq)
    def _(t):
        at = pl.ds(pl.multiple_of(t * tq, tq), tq)
        dqt[:, at] = dot(kt[...], ut[:, at])

    factors(0)

    tb = ny * tok

    @pl.loop(0, nx)
    def _(t):
        at = pl.ds(pl.multiple_of(t * tb, tb), tb)
        dk_acc[at, :] = dot(ut[at, 0:half], qs[0:half, :])
        dv_acc[at, :] = dot(et[at, 0:half], gs[0:half, :])

    factors(1)
    dqr[me_q] = dqs[mine_q, :]

    def kv_block(j, s, n):
        src, dst = ((dks, dkr), (dvs, dvr))[j]
        device = at_xy(s // ny, lax.rem(s, ny))
        return send(src.at[rows_of(s), :], dst.at[n], k_send.at[1 + j, s], k_recv.at[1 + j, n], device)

    def grad_tiles(j):
        out, acc, left, right = ((dks, dk_acc, ut, qs), (dvs, dv_acc, et, gs))[j]

        def step(i, carry):
            t = lax.rem(x + 2 + i, nx)
            at = pl.ds(pl.multiple_of(t * tb, tb), tb)
            out[at, :] = (acc[at, :] + dot(left[at, half:], right[half:, :])).astype(bf16)
            for b in range(ny):
                s = t * ny + b

                @pl.when(s != me_k)
                def _():
                    kv_block(j, s, me_k).start()

            return carry

        lax.fori_loop(0, nx, step, 0)

    def summed(ref):
        acc = ref[0].astype(f32)
        for s in range(1, ref.shape[0]):
            acc = acc + ref[s].astype(f32)
        return acc

    def g_block(j, s, device, sem, n):
        ref = gr.at[s, 0:tok, 128 * j : 128 * j + 128]
        return send(ref, ref, sem.at[j, n], p_recv.at[j, s], device)

    def send_grad(j, ref, out):
        value = summed(ref).astype(bf16)
        out[...] = value
        gr[me_p, 0:tok, 128 * j : 128 * j + 128] = value
        each_y(lambda b: g_block(j, me_p, (x, zl, zh, b, c), p_send, b).start())
        g_block(j, me_p, partner, h_send, y).start()

    def w_block(j, s, n):
        return send(ws.at[j, s], wr.at[j, n], w_send.at[j, s], w_recv.at[j, n], at_zh(s))

    def send_weight(j):
        def land(b):
            s = b * nc + c
            g_block(j, s, partner, h_send, b).wait_recv()
            g_block(j, s, partner, h_send, b).start()

        each_y(land)

        def land_rest(b, carry):
            g_block(j, b * nc + other, partner, h_send, b).wait_recv()
            return carry

        lax.fori_loop(0, ny, land_rest, 0)
        acc = dot(xr[0], gr[0, :, 128 * j : 128 * j + 128])
        for p in range(1, npc):
            acc = acc + dot(xr[p], gr[p, :, 128 * j : 128 * j + 128])
        for n in range(nzh):
            ws[j, n] = acc[n * chunk : (n + 1) * chunk, :].astype(bf16)
        each(zh, nzh, lambda s: w_block(j, s, zh).start())
        wr[j, zh] = ws[j, zh]

    def a_block(j, s, n):
        return send(ar.at[j, n], ar.at[j, n], a_send.at[j, s], a_recv.at[j, n], at_r(s))

    def send_rows(j):
        each(zh, nzh, lambda s: w_block(j, s, s).wait_recv())
        ar[j, me_r] = summed(wr.at[j]).astype(bf16)
        each(me_r, nr, lambda s: a_block(j, s, me_r).start())

    def finish(j):
        each(me_r, nr, lambda s: a_block(j, s, s).wait_recv())
        wg_out[:, 128 * j : 128 * j + 128] = summed(ar.at[j])

    grad_tiles(0)
    dkr[me_k] = dks[mine_k, :]
    grad_tiles(1)
    dvr[me_k] = dvs[mine_k, :]
    each(me_q, nq, lambda s: dq_block(s, s).wait_recv())
    send_grad(0, dqr, dq_out)
    own.wait()
    each(me_p, npc, lambda s: x_block(s, s).wait_recv())
    each(me_k, nk, lambda s: kv_block(0, s, s).wait_recv())
    send_grad(1, dkr, dk_out)
    send_weight(0)
    each(me_k, nk, lambda s: kv_block(1, s, s).wait_recv())
    send_grad(2, dvr, dv_out)
    send_weight(1)
    send_rows(0)
    send_weight(2)
    send_rows(1)
    finish(0)
    send_rows(2)
    finish(1)
    finish(2)

    def q_left(w):
        for copy in q_block(me_q, partner, q_send, w):
            copy.wait_send()

    each_z(q_left)

    def f_left(w, carry):
        for copy in q_block(me_q, partner, f_send, w):
            copy.wait_send()
        return carry

    lax.fori_loop(0, nz, f_left, 0)

    def st_left(s):
        for h in range(2):
            st_block(h, me_q, partner, s).wait_send()
        dq_block(s, me_q).wait_send()

    each(me_q, nq, st_left)

    def k_left(s):
        k_block(me_k, partner, s).wait_send()
        for j in range(2):
            kv_block(j, s, me_k).wait_send()

    each(me_k, nk, k_left)
    each(me_p, npc, lambda s: x_block(s, me_p).wait_send())

    for j in range(3):
        each_y(lambda b: g_block(j, me_p, partner, p_send, b).wait_send())

        def h_left(b, carry):
            g_block(j, me_p, partner, h_send, b).wait_send()
            return carry

        lax.fori_loop(0, ny, h_left, 0)
        each(zh, nzh, lambda s: w_block(j, s, zh).wait_send())
        each(me_r, nr, lambda s: a_block(j, s, me_r).wait_send())


def local(
    dims, layer_input, queries, key_states, value_states, forward_out, out_grad, token_pos,
    block_sample,
):
    nx, nzl, nzh, ny, nc = dims
    tok, width = queries.shape
    depth = layer_input.shape[1]
    chunk = depth // (nzh * ny * nc)
    nq, nk, npc, nr = nzh * nzl * nc, nx * ny, ny * nc, nx * nzl
    n_query, n_key = nq * tok, nk * tok
    pos = token_pos.reshape(-1, tok)
    blocks = block_sample.reshape(1, -1)
    nz = nzh * nzl
    V = pltpu.VMEM
    dma = pltpu.SemaphoreType.DMA
    scratch = [
        V((n_query, 256), bf16), V((nq, 1, 256), f32), V((n_key, 256), bf16),
        V((n_query, 128), bf16), V((n_key, 128), bf16), V((128, n_key), bf16),
        V((n_key, n_query), bf16), V((n_key, n_query), bf16), V((n_key, 256), f32),
        V((128, n_query), f32), V((2, nq, 2, n_query // 2), f32), V((8, n_query), f32),
        V((n_query, 128), bf16), V((n_query, 128), bf16),
        V((n_key, 128), f32), V((n_key, 128), f32),
        V((n_query, 128), bf16), V((nq, tok, 128), bf16),
        V((n_key, 128), bf16), V((n_key, 128), bf16),
        V((nk, tok, 128), bf16), V((nk, tok, 128), bf16),
        V((npc, nzh * chunk, 256), bf16), V((npc, nzh * chunk, 256), bf16),
        V((npc, 256, 384), bf16), V((3, nzh, chunk, 128), bf16), V((3, nzh, chunk, 128), bf16),
        V((3, nr, chunk, 128), bf16),
        dma((3, nq)), dma((3, nq)), dma((2, nz)), dma((2, nq)), dma((2, nq)),
        dma((3, nk)), dma((3, nk)), dma((npc,)), dma((npc,)),
        dma((3, ny)), dma((3, ny)), dma((3, npc)),
        dma((3, nzh)), dma((3, nzh)), dma((3, nr)), dma((3, nr)), dma,
    ]

    def body(*refs):
        kernel(dims, *refs)

    vmem = pl.BlockSpec(memory_space=pltpu.VMEM)
    grad = jax.ShapeDtypeStruct((tok, 128), bf16)
    return pl.pallas_call(
        body,
        out_shape=(grad, grad, grad, jax.ShapeDtypeStruct((chunk, 384), f32)),
        in_specs=[vmem] * 8,
        out_specs=(vmem,) * 4,
        scratch_shapes=scratch,
        compiler_params=pltpu.CompilerParams(
            collective_id=0, has_side_effects=True, vmem_limit_bytes=64 * 2**20
        ),
        name="packed_backward",
    )(queries, key_states, value_states, forward_out, out_grad, layer_input, pos, blocks)


def on_mesh(finer):
    dims = tuple(finer.shape[a] for a in AXES)
    slots, cols = P(AXES, None), P(("zh", "y", "c"), None)
    return jax.shard_map(
        lambda *args: local(dims, *args),
        mesh=finer,
        in_specs=(slots,) * 6 + (P(), P()),
        out_specs=(slots, slots, slots, cols),
        check_vma=False,
    )


def solution(mesh):
    return on_mesh(Mesh(mesh.devices.reshape(4, 2, 4, 4, 2), AXES))
```

```python
import math

import jax
import jax.numpy as jnp
from jax import lax
from jax.experimental import pallas as pl
from jax.experimental.pallas import tpu as pltpu
from jax.sharding import Mesh
from jax.sharding import PartitionSpec as P

BLK = 128
BIG = 16384.0
MESH = pl.DeviceIdType.MESH
NT = (((1,), (1,)), ((), ()))
AXES = ("x", "zl", "zh", "y", "c")
bf16 = jnp.bfloat16
f32 = jnp.float32


def dot_nt(a, b, **kw):
    return lax.dot_general(a, b, NT, preferred_element_type=f32, **kw)


def dot(a, b):
    return jnp.dot(a, b, preferred_element_type=f32)


def as_column(row):
    return jnp.transpose(jnp.broadcast_to(row, (128, row.shape[1])))


def eye(n):
    return (
        lax.broadcasted_iota(jnp.int32, (n, n), 0) == lax.broadcasted_iota(jnp.int32, (n, n), 1)
    ).astype(bf16)


def by_distance(n):
    return sorted(range(1, n), key=lambda d: -min(d, n - d))


def kernel(
    dims, q_in, k_in, v_in, o_in, g_in, x_in, pos_ref, block_ref,
    dq_out, dk_out, dv_out, wg_out,
    qb, gb, ob, db, kb, vb, xb, pos, blocks, column, fq, fk, kt, et, ut, s_scr, dqt, st, rr, gs, qs,
    dqs, dqp, dqc, dqr, dks, dvs, dkr, dvr, xt, xr, gr, ws, wr, ar, wg,
    q_send, q_recv, f_send, t_send, t_recv, e_send, e_recv, d_send, d_recv, k_send, k_recv,
    x_send, x_recv, p_send, h_send, p_recv, w_send, w_recv, a_send, a_recv, own_sem, in_sem, out_sem,
):
    nx, nzl, nzh, ny, nc = dims
    tok = q_in.shape[0]
    chunk = wg_out.shape[0]
    n_block = block_ref.shape[0]
    x, zl, zh, y, c = (lax.axis_index(a) for a in AXES)
    nz = nzh * nzl
    nq, nk, npc, nr = nz * nc, nx * ny, ny * nc, nx * nzl
    z = zh * nzl + zl
    me_q = z * nc + c
    me_k = x * ny + y
    me_p = y * nc + c
    me_r = x * nzl + zl
    n_query, n_key = nq * tok, nk * tok
    half = n_query // 2

    def rows_of(s):
        return pl.ds(pl.multiple_of(s * tok, tok), tok)

    def at_z(w, core):
        return (x, lax.rem(w, nzl), w // nzl, y, core)

    def at_xy(a, b):
        return (a, zl, zh, b, c)

    def at_p(s):
        return (x, zl, zh, s // nc, lax.rem(s, nc))

    def at_zh(s):
        return (x, zl, s, y, c)

    def at_r(s):
        return (s // nzl, lax.rem(s, nzl), zh, y, c)

    other = 1 - c
    partner = (x, zl, zh, y, other)

    def send(src, dst, send_sem, recv_sem, device):
        return pltpu.make_async_remote_copy(
            src_ref=src, dst_ref=dst, send_sem=send_sem, recv_sem=recv_sem,
            device_id=device, device_id_type=MESH,
        )

    def each(me, size, body):
        def step(i, carry):
            body(lax.rem(me + i, size))
            return carry

        lax.fori_loop(1, size, step, 0)

    def each_z(body):
        for d in by_distance(nz):
            body(lax.rem(z + d, nz))

    def each_y(body):
        for d in by_distance(ny):
            body(lax.rem(y + d, ny))

    def each_xy(body):
        pairs = [(a, b) for a in range(nx) for b in range(ny) if a or b]
        for a, b in sorted(pairs, key=lambda p: -min(p[0], nx - p[0]) - min(p[1], ny - p[1])):
            body(lax.rem(x + a, nx), lax.rem(y + b, ny))

    mine_q, mine_k = rows_of(me_q), rows_of(me_k)
    staged = [
        pltpu.make_async_copy(src, dst, in_sem.at[i])
        for i, (src, dst) in enumerate(
            (
                (k_in, kb.at[mine_k, :]), (q_in, qb.at[mine_q, :]), (v_in, vb.at[mine_k, :]),
                (g_in, gb.at[mine_q, :]), (o_in, ob), (pos_ref, pos), (block_ref, blocks), (x_in, xb),
            )
        )
    ]
    for copy in staged:
        copy.start()

    barrier = pltpu.get_barrier_semaphore()

    def hello(device):
        pl.semaphore_signal(barrier, inc=1, device_id=device, device_id_type=MESH)

    each(me_q, nq, lambda s: hello(at_z(s // nc, lax.rem(s, nc))))
    each(me_k, nk, lambda s: hello(at_xy(s // ny, lax.rem(s, ny))))
    each(me_p, npc, lambda s: hello(at_p(s)))
    each(zh, nzh, lambda s: hello(at_zh(s)))
    each(me_r, nr, lambda s: hello(at_r(s)))

    for copy in staged[:5]:
        copy.wait()
    product = gb[mine_q, :].astype(f32) * ob[...].astype(f32)
    delta = dot_nt(jnp.ones((8, product.shape[1]), f32), product, precision=lax.Precision.HIGHEST)
    db[me_q, :, 0:tok] = delta[0:1, :]
    pl.semaphore_wait(barrier, nq + nk + npc + nzh + nr - 5)

    def q_block(m, s, device, sem, n):
        ref = (qb.at[rows_of(s), :], gb.at[rows_of(s), :], db.at[s])[m]
        return send(ref, ref, sem.at[m, n], q_recv.at[m, s], device)

    def k_block(m, s, device, n):
        ref = (kb, vb)[m].at[rows_of(s), :]
        return send(ref, ref, k_send.at[m, n], k_recv.at[m, s], device)

    def start_q(m):
        each_z(lambda w: q_block(m, me_q, at_z(w, c), q_send, w).start())
        q_block(m, me_q, partner, f_send, z).start()

    def start_k(m):
        each_xy(lambda a, b: k_block(m, me_k, at_xy(a, b), a * ny + b).start())

    def hand_on(m):
        def land(w):
            s = w * nc + c
            q_block(m, s, partner, f_send, w).wait_recv()
            q_block(m, s, partner, f_send, w).start()

        each_z(land)

    def land_q(m):
        def land(w, carry):
            q_block(m, w * nc + other, partner, f_send, w).wait_recv()
            return carry

        lax.fori_loop(0, nz, land, 0)

    def land_k(m):
        each_xy(lambda a, b: k_block(m, a * ny + b, at_xy(a, b), a * ny + b).wait_recv())

    start_q(0)
    start_k(0)
    start_q(2)
    start_q(1)
    start_k(1)

    for copy in staged[5:]:
        copy.wait()
    samples = lax.broadcasted_iota(jnp.int32, (1, 128), 1)

    def count(b, carry):
        below, upto = carry
        sample = blocks[b]
        return (
            below + jnp.where(sample < samples, float(BLK), 0.0),
            upto + jnp.where(sample <= samples, float(BLK), 0.0),
        )

    none = jnp.zeros((1, 128), f32)
    low, high = lax.fori_loop(0, n_block, count, (none, none))
    last = lax.broadcasted_iota(jnp.int32, (tok, 128), 1) == 127

    def one_hot(device, hit, always):
        index = device[0]
        for n, i in zip(dims[1:], device[1:]):
            index = index * n + i
        first = index * tok // 128
        skip = pl.multiple_of(lax.rem(index * tok, 128), 32)
        row = jnp.concatenate([pos[pl.ds(first, 1), :], pos[pl.ds(first + 1, 1), :]], axis=1)
        column[...] = as_column(row.astype(f32))
        col = column[pl.ds(skip, tok), :]
        inside = jnp.where((col >= low) & (col < high), hit, 0.0)
        return jnp.where(last, always, inside).astype(bf16)

    def query_hot(s, carry):
        fq[rows_of(s), :] = one_hot(at_z(s // nc, lax.rem(s, nc)), BIG, -BIG)
        return carry

    def key_hot(s, carry):
        fk[rows_of(s), :] = one_hot(at_xy(s // ny, lax.rem(s, ny)), 1.0, 1.0)
        return carry

    lax.fori_loop(0, nk, key_hot, 0)

    hand_on(0)
    lax.fori_loop(0, nq, query_hot, 0)

    xt[:, :, tok:] = jnp.zeros((npc, nzh * chunk, 256 - tok), bf16)
    gr[:, tok:, :] = jnp.zeros((npc, 256 - tok, 384), bf16)
    four = eye(4 * chunk)
    for g in range(nzh * npc // 4):
        turned = dot_nt(four, xb[:, g * 4 * chunk : (g + 1) * 4 * chunk]).astype(bf16)
        for j in range(4):
            n = 4 * g + j
            rows = slice(n // npc * chunk, (n // npc + 1) * chunk)
            xt[n % npc, rows, 0:tok] = turned[j * chunk : (j + 1) * chunk, :]

    land_k(0)
    land_q(0)

    def x_block(s, n):
        return send(xt.at[s], xr.at[n], x_send.at[s], x_recv.at[n], at_p(s))

    own = pltpu.make_async_copy(xt.at[me_p], xr.at[me_p], own_sem)
    own.start()
    each(me_p, npc, lambda s: x_block(s, me_p).start())

    tq = 256 if half % 256 == 0 else 128
    tk = 256 if n_key % 256 == 0 else tok
    score_scale = 1.0 / math.sqrt(128.0)
    rate = score_scale / math.log(2.0)
    kt[...] = dot_nt(eye(128), kb[...]).astype(bf16)

    def tile(t):
        return pl.ds(pl.multiple_of(t * tq, tq), tq)

    def score_tile(t):
        at = tile(t)
        query_tile = jnp.concatenate([qb[at, :], fq[at, :]], axis=1)
        top = jnp.full((8, tq), -3.0e38, f32)
        for n in range(n_key // tk):
            span = slice(n * tk, (n + 1) * tk)
            s = dot_nt(jnp.concatenate([kb[span, :], fk[span, :]], axis=1), query_tile)
            s_scr[span, 0:tq] = s
            top = jnp.maximum(top, jnp.max(s.reshape(tk // 8, 8, tq), axis=0))
        peak = jnp.max(top, axis=0, keepdims=True)
        total = jnp.zeros((8, tq), f32)
        for n in range(n_key // tk):
            span = slice(n * tk, (n + 1) * tk)
            e = jnp.exp2((s_scr[span, 0:tq] - peak) * rate)
            total = total + jnp.sum(e.reshape(tk // 8, 8, tq), axis=0)
            et[span, at] = e.astype(bf16)
        rr[0:1, at] = peak
        rr[1:2, at] = jnp.sum(total, axis=0, keepdims=True)

    def grad_tile(t):
        at = tile(t)
        grad_rows = gb[at, :]
        delta_row = rr[2:3, at]
        acc = jnp.zeros((128, tq), f32)
        for n in range(n_key // tk):
            span = slice(n * tk, (n + 1) * tk)
            slope = dot_nt(vb[span, :], grad_rows) - delta_row
            u = (et[span, at].astype(f32) * slope).astype(bf16)
            ut[span, at] = u
            acc = acc + dot(kt[:, span], u)
        dqt[:, at] = acc

    def st_block(h, s, device, n):
        return send(st.at[h, s], st.at[h, s], t_send.at[h, n], t_recv.at[h, s], device)

    def send_stats(h):
        st[h, me_q] = rr[0:2, h * half : (h + 1) * half]
        each(me_q, nq, lambda s: st_block(h, me_q, at_z(s // nc, lax.rem(s, nc)), s).start())

    def factors(h):
        each(me_q, nq, lambda s: st_block(h, s, partner, s).wait_recv())
        part = slice(h * half, (h + 1) * half)
        peak = st[h, 0, 0:1, :]
        for s in range(1, nq):
            peak = jnp.maximum(peak, st[h, s, 0:1, :])
        total = jnp.zeros_like(peak)
        for s in range(nq):
            total = total + st[h, s, 1:2, :] * jnp.exp2((st[h, s, 0:1, :] - peak) * rate)
        rr[3:4, part] = jnp.exp2((rr[0:1, part] - peak) * rate) / total

    def scale_rows(t):
        at = tile(t)
        factor = rr[3:4, at]
        dqs[at, :] = jnp.transpose(dqt[:, at] * (factor * score_scale)).astype(bf16)
        col = as_column(factor)
        gs[at, :] = (gb[at, :].astype(f32) * col).astype(bf16)
        qs[at, :] = (qb[at, :].astype(f32) * (col * score_scale)).astype(bf16)

    tiles = n_query // tq
    most = tiles - max(1, tiles // 5)
    pl.loop(0, tiles // 2)(score_tile)
    send_stats(0)
    pl.loop(tiles // 2, most)(score_tile)
    hand_on(2)
    hand_on(1)
    pl.loop(most, tiles)(score_tile)
    send_stats(1)
    land_k(1)
    land_q(2)
    land_q(1)
    rr[2:3, :] = jnp.concatenate([db[s, :, 0:tok] for s in range(nq)], axis=1)
    pl.loop(0, tiles)(grad_tile)
    factors(0)
    factors(1)
    pl.loop(0, tiles)(scale_rows)

    def pair_block(w, core):
        src = dqs.at[rows_of(w * nc + core), :]
        return send(src, dqp.at[w], e_send.at[w], e_recv.at[w], partner)

    def dq_block(w, n):
        return send(dqc.at[w], dqr.at[n], d_send.at[w], d_recv.at[n], at_z(w, c))

    def send_pair(w, carry):
        pair_block(w, other).start()
        return carry

    lax.fori_loop(0, nz, send_pair, 0)

    def send_dq():
        def add(w):
            pair_block(w, c).wait_recv()
            mine = dqs[rows_of(w * nc + c), :].astype(f32)
            dqc[w] = (mine + dqp[w].astype(f32)).astype(bf16)

        def step(w):
            add(w)
            dq_block(w, z).start()

        each_z(step)
        add(z)
        dqr[z] = dqc[z]

    tb = ny * tok

    def kv_block(j, s, n):
        src, dst = ((dks, dkr), (dvs, dvr))[j]
        device = at_xy(s // ny, lax.rem(s, ny))
        return send(src.at[rows_of(s), :], dst.at[n], k_send.at[2 + j, s], k_recv.at[2 + j, n], device)

    def grad_tiles(j, first, end):
        out, left, right = ((dks, ut, qs), (dvs, et, gs))[j]

        def step(i, carry):
            t = lax.rem(x + 2 + i, nx)
            at = pl.ds(pl.multiple_of(t * tb, tb), tb)
            out[at, :] = dot(left[at, :], right[...]).astype(bf16)
            for b in range(ny):
                s = t * ny + b

                @pl.when(s != me_k)
                def _():
                    kv_block(j, s, me_k).start()

            return carry

        lax.fori_loop(first, end, step, 0)

    def summed(ref):
        acc = ref[0].astype(f32)
        for s in range(1, ref.shape[0]):
            acc = acc + ref[s].astype(f32)
        return acc

    def g_block(j, s, device, sem, n):
        ref = gr.at[s, 0:tok, 128 * j : 128 * j + 128]
        return send(ref, ref, sem.at[j, n], p_recv.at[j, s], device)

    def grad_out(j):
        src = gr.at[me_p, 0:tok, 128 * j : 128 * j + 128]
        return pltpu.make_async_copy(src, (dq_out, dk_out, dv_out)[j], out_sem.at[j])

    def send_grad(j, ref):
        gr[me_p, 0:tok, 128 * j : 128 * j + 128] = summed(ref).astype(bf16)
        each_y(lambda b: g_block(j, me_p, (x, zl, zh, b, c), p_send, b).start())
        g_block(j, me_p, partner, h_send, y).start()
        grad_out(j).start()

    def w_block(j, s, n):
        return send(ws.at[j, s], wr.at[j, n], w_send.at[j, s], w_recv.at[j, n], at_zh(s))

    def send_weight(j):
        def land(b):
            s = b * nc + c
            g_block(j, s, partner, h_send, b).wait_recv()
            g_block(j, s, partner, h_send, b).start()

        each_y(land)

        def land_rest(b, carry):
            g_block(j, b * nc + other, partner, h_send, b).wait_recv()
            return carry

        lax.fori_loop(0, ny, land_rest, 0)
        acc = dot(xr[0], gr[0, :, 128 * j : 128 * j + 128])
        for p in range(1, npc):
            acc = acc + dot(xr[p], gr[p, :, 128 * j : 128 * j + 128])
        for n in range(nzh):
            ws[j, n] = acc[n * chunk : (n + 1) * chunk, :].astype(bf16)
        each(zh, nzh, lambda s: w_block(j, s, zh).start())
        wr[j, zh] = ws[j, zh]

    def a_block(j, s, n):
        return send(ar.at[j, n], ar.at[j, n], a_send.at[j, s], a_recv.at[j, n], at_r(s))

    def send_rows(j):
        each(zh, nzh, lambda s: w_block(j, s, s).wait_recv())
        ar[j, me_r] = summed(wr.at[j]).astype(bf16)
        each(me_r, nr, lambda s: a_block(j, s, me_r).start())

    def weight_out(j):
        lanes = slice(128 * j, 128 * j + 128)
        return pltpu.make_async_copy(wg.at[:, lanes], wg_out.at[:, lanes], out_sem.at[3 + j])

    def finish(j):
        each(me_r, nr, lambda s: a_block(j, s, s).wait_recv())
        wg[:, 128 * j : 128 * j + 128] = summed(ar.at[j])
        weight_out(j).start()

    grad_tiles(1, 0, 1)
    send_dq()
    grad_tiles(1, 1, nx)
    dvr[me_k] = dvs[mine_k, :]
    grad_tiles(0, 0, nx)
    dkr[me_k] = dks[mine_k, :]
    each_z(lambda w: dq_block(w, w).wait_recv())
    send_grad(0, dqr)
    own.wait()
    each(me_p, npc, lambda s: x_block(s, s).wait_recv())
    each(me_k, nk, lambda s: kv_block(1, s, s).wait_recv())
    send_grad(2, dvr)
    send_weight(0)
    each(me_k, nk, lambda s: kv_block(0, s, s).wait_recv())
    send_grad(1, dkr)
    send_weight(2)
    send_rows(0)
    send_weight(1)
    send_rows(2)
    finish(0)
    send_rows(1)
    finish(2)
    finish(1)

    for m in range(3):
        each_z(lambda w: q_block(m, me_q, partner, q_send, w).wait_send())

        def f_left(w, carry):
            q_block(m, me_q, partner, f_send, w).wait_send()
            return carry

        lax.fori_loop(0, nz, f_left, 0)

    def st_left(s):
        for h in range(2):
            st_block(h, me_q, partner, s).wait_send()

    each(me_q, nq, st_left)

    def pair_left(w, carry):
        pair_block(w, other).wait_send()
        return carry

    lax.fori_loop(0, nz, pair_left, 0)
    each_z(lambda w: dq_block(w, z).wait_send())

    def k_left(s):
        for j in range(2):
            k_block(j, me_k, partner, s).wait_send()
            kv_block(j, s, me_k).wait_send()

    each(me_k, nk, k_left)
    each(me_p, npc, lambda s: x_block(s, me_p).wait_send())

    for j in range(3):
        each_y(lambda b: g_block(j, me_p, partner, p_send, b).wait_send())

        def h_left(b, carry):
            g_block(j, me_p, partner, h_send, b).wait_send()
            return carry

        lax.fori_loop(0, ny, h_left, 0)
        each(zh, nzh, lambda s: w_block(j, s, zh).wait_send())
        each(me_r, nr, lambda s: a_block(j, s, me_r).wait_send())
        grad_out(j).wait()
        weight_out(j).wait()


def local(
    dims, layer_input, queries, key_states, value_states, forward_out, out_grad, token_pos,
    block_sample,
):
    nx, nzl, nzh, ny, nc = dims
    tok = queries.shape[0]
    depth = layer_input.shape[1]
    chunk = depth // (nzh * ny * nc)
    nq, nk, npc, nr = nzh * nzl * nc, nx * ny, ny * nc, nx * nzl
    n_query, n_key = nq * tok, nk * tok
    pos = token_pos.reshape(-1, 128)
    nz = nzh * nzl
    V = pltpu.VMEM
    dma = pltpu.SemaphoreType.DMA
    scratch = [
        V((n_query, 128), bf16), V((n_query, 128), bf16), V((tok, 128), bf16), V((nq, 1, 256), f32),
        V((n_key, 128), bf16), V((n_key, 128), bf16), V((tok, depth), bf16),
        V(pos.shape, jnp.int32), pltpu.SMEM(block_sample.shape, jnp.int32), V((256, 128), f32),
        V((n_query, 128), bf16), V((n_key, 128), bf16), V((128, n_key), bf16),
        V((n_key, n_query), bf16), V((n_key, n_query), bf16), V((n_key, 256), f32),
        V((128, n_query), f32), V((2, nq, 2, n_query // 2), f32), V((8, n_query), f32),
        V((n_query, 128), bf16), V((n_query, 128), bf16),
        V((n_query, 128), bf16), V((nz, tok, 128), bf16), V((nz, tok, 128), bf16),
        V((nz, tok, 128), bf16),
        V((n_key, 128), bf16), V((n_key, 128), bf16),
        V((nk, tok, 128), bf16), V((nk, tok, 128), bf16),
        V((npc, nzh * chunk, 256), bf16), V((npc, nzh * chunk, 256), bf16),
        V((npc, 256, 384), bf16), V((3, nzh, chunk, 128), bf16), V((3, nzh, chunk, 128), bf16),
        V((3, nr, chunk, 128), bf16), V((chunk, 384), f32),
        dma((3, nz)), dma((3, nq)), dma((3, nz)), dma((2, nq)), dma((2, nq)),
        dma((nz,)), dma((nz,)), dma((nz,)), dma((nz,)),
        dma((4, nk)), dma((4, nk)), dma((npc,)), dma((npc,)),
        dma((3, ny)), dma((3, ny)), dma((3, npc)),
        dma((3, nzh)), dma((3, nzh)), dma((3, nr)), dma((3, nr)), dma, dma((8,)), dma((6,)),
    ]

    def body(*refs):
        kernel(dims, *refs)

    hbm = pl.BlockSpec(memory_space=pl.ANY)
    grad = jax.ShapeDtypeStruct((tok, 128), bf16)
    return pl.pallas_call(
        body,
        out_shape=(grad, grad, grad, jax.ShapeDtypeStruct((chunk, 384), f32)),
        in_specs=[hbm] * 8,
        out_specs=(hbm,) * 4,
        scratch_shapes=scratch,
        compiler_params=pltpu.CompilerParams(
            collective_id=0, has_side_effects=True, vmem_limit_bytes=64 * 2**20
        ),
        name="packed_backward",
    )(queries, key_states, value_states, forward_out, out_grad, layer_input, pos, block_sample)


def on_mesh(finer):
    dims = tuple(finer.shape[a] for a in AXES)
    slots, cols = P(AXES, None), P(("zh", "y", "c"), None)
    return jax.shard_map(
        lambda *args: local(dims, *args),
        mesh=finer,
        in_specs=(slots,) * 6 + (P(), P()),
        out_specs=(slots, slots, slots, cols),
        check_vma=False,
    )


def solution(mesh):
    return on_mesh(Mesh(mesh.devices.reshape(4, 2, 4, 4, 2), AXES))
```

```python
import math

import jax
import jax.numpy as jnp
from jax import lax
from jax.experimental import pallas as pl
from jax.experimental.pallas import tpu as pltpu
from jax.sharding import Mesh
from jax.sharding import PartitionSpec as P

BLK = 128
BIG = 16384.0
MESH = pl.DeviceIdType.MESH
NT = (((1,), (1,)), ((), ()))
AXES = ("x", "zl", "zh", "y", "c")
bf16 = jnp.bfloat16
f32 = jnp.float32


def dot_nt(a, b, **kw):
    return lax.dot_general(a, b, NT, preferred_element_type=f32, **kw)


def dot(a, b):
    return jnp.dot(a, b, preferred_element_type=f32)


def as_column(row):
    return jnp.transpose(jnp.broadcast_to(row, (128, row.shape[1])))


def eye(n):
    return (
        lax.broadcasted_iota(jnp.int32, (n, n), 0) == lax.broadcasted_iota(jnp.int32, (n, n), 1)
    ).astype(bf16)


def by_distance(n):
    return sorted(range(1, n), key=lambda d: -min(d, n - d))


def near(i):
    return i + i // 2 - 2 * (i // 3)


def kernel(
    dims, q_in, k_in, v_in, o_in, g_in, x_in, pos_ref, block_ref,
    dq_out, dk_out, dv_out, wg_out,
    qb, gb, ob, db, kb, vb, xb, pos, blocks, column, fq, fk, kt, et, ut, s_scr, dqt, st, pk, lk, wk, rr,
    gs, qs,
    dqs, dqp, dqc, dqr, dks, dvs, dkr, dvr, xt, xr, gr, ws, wr, ar, wg,
    q_send, q_recv, f_send, e_send, e_recv, d_send, d_recv, k_send, k_recv,
    x_send, x_recv, p_send, h_send, p_recv, w_send, w_recv, a_send, a_recv, own_sem, in_sem, out_sem,
):
    nx, nzl, nzh, ny, nc = dims
    tok = q_in.shape[0]
    chunk = wg_out.shape[0]
    n_block = block_ref.shape[0]
    x, zl, zh, y, c = (lax.axis_index(a) for a in AXES)
    nz = nzh * nzl
    nq, nk, npc, nr = nz * nc, nx * ny, ny * nc, nx * nzl
    z = zh * nzl + zl
    me_q = z * nc + c
    me_k = x * ny + y
    me_p = y * nc + c
    me_r = x * nzl + zl
    n_query, n_key = nq * tok, nk * tok
    key_chunk, query_chunk = ny * tok, nzl * nc * tok

    def rows_of(s):
        return pl.ds(pl.multiple_of(s * tok, tok), tok)

    def at_z(w, core):
        return (x, lax.rem(w, nzl), w // nzl, y, core)

    def at_xy(a, b):
        return (a, zl, zh, b, c)

    def at_p(s):
        return (x, zl, zh, s // nc, lax.rem(s, nc))

    def at_zh(s):
        return (x, zl, s, y, c)

    def at_r(s):
        return (s // nzl, lax.rem(s, nzl), zh, y, c)

    other = 1 - c
    partner = (x, zl, zh, y, other)

    def send(src, dst, send_sem, recv_sem, device):
        return pltpu.make_async_remote_copy(
            src_ref=src, dst_ref=dst, send_sem=send_sem, recv_sem=recv_sem,
            device_id=device, device_id_type=MESH,
        )

    def each(me, size, body):
        def step(i, carry):
            body(lax.rem(me + i, size))
            return carry

        lax.fori_loop(1, size, step, 0)

    def each_z(body):
        for d in by_distance(nz):
            body(lax.rem(z + d, nz))

    def each_y(body):
        for d in by_distance(ny):
            body(lax.rem(y + d, ny))

    def each_xy(body):
        for i in range(nx):
            for n in range(ny):
                if i or n:
                    body(lax.rem(x + nx - near(i), nx), lax.rem(y + ny - near(n), ny))

    def chunk_z(i, body):
        h = lax.rem(zh + near(i), nzh)
        for n in range(nzl):
            w = h * nzl + n
            if i:
                body(w)
            else:
                pl.when(w != z)(lambda w=w: body(w))

    mine_q, mine_k = rows_of(me_q), rows_of(me_k)
    staged = [
        pltpu.make_async_copy(src, dst, in_sem.at[i])
        for i, (src, dst) in enumerate(
            (
                (k_in, kb.at[mine_k, :]), (q_in, qb.at[mine_q, :]), (v_in, vb.at[mine_k, :]),
                (g_in, gb.at[mine_q, :]), (o_in, ob), (pos_ref, pos), (block_ref, blocks), (x_in, xb),
            )
        )
    ]
    for copy in staged:
        copy.start()

    barrier = pltpu.get_barrier_semaphore()

    def hello(device):
        pl.semaphore_signal(barrier, inc=1, device_id=device, device_id_type=MESH)

    each(me_q, nq, lambda s: hello(at_z(s // nc, lax.rem(s, nc))))
    each(me_k, nk, lambda s: hello(at_xy(s // ny, lax.rem(s, ny))))
    each(me_p, npc, lambda s: hello(at_p(s)))
    each(zh, nzh, lambda s: hello(at_zh(s)))
    each(me_r, nr, lambda s: hello(at_r(s)))

    for copy in staged[:5]:
        copy.wait()
    product = gb[mine_q, :].astype(f32) * ob[...].astype(f32)
    delta = dot_nt(jnp.ones((8, product.shape[1]), f32), product, precision=lax.Precision.HIGHEST)
    db[me_q, :, 0:tok] = delta[0:1, :]
    pl.semaphore_wait(barrier, nq + nk + npc + nzh + nr - 5)

    def q_block(m, s, device, sem, n):
        ref = (qb.at[rows_of(s), :], gb.at[rows_of(s), :], db.at[s], st.at[s])[m]
        return send(ref, ref, sem.at[m, n], q_recv.at[m, s], device)

    def k_block(m, s, device, n):
        ref = (kb, vb)[m].at[rows_of(s), :]
        return send(ref, ref, k_send.at[m, n], k_recv.at[m, s], device)

    def start_q(m):
        for i in range(nzh):
            h = lax.rem(zh + nzh - near(i), nzh)
            for n in range(nzl):
                w = h * nzl + n
                copy = q_block(m, me_q, at_z(w, c), q_send, w)
                if i:
                    copy.start()
                else:
                    pl.when(w != z)(copy.start)
        q_block(m, me_q, partner, f_send, z).start()

    def start_k(m):
        each_xy(lambda a, b: k_block(m, me_k, at_xy(a, b), a * ny + b).start())

    def hand_on(m, i):
        def land(w):
            s = w * nc + c
            q_block(m, s, partner, f_send, w).wait_recv()
            q_block(m, s, partner, f_send, w).start()

        chunk_z(i, land)

    def land_q(m, i):
        h = lax.rem(zh + near(i), nzh)
        for n in range(nzl):
            w = h * nzl + n
            q_block(m, w * nc + other, partner, f_send, w).wait_recv()

    def land_k(m, i):
        a = lax.rem(x + near(i), nx)
        for n in range(ny):
            if i or n:
                s = a * ny + lax.rem(y + near(n), ny)
                k_block(m, s, partner, s).wait_recv()

    start_q(0)
    start_k(0)
    start_q(2)
    start_q(1)
    start_k(1)

    for copy in staged[5:]:
        copy.wait()
    samples = lax.broadcasted_iota(jnp.int32, (1, 128), 1)

    def count(b, carry):
        below, upto = carry
        sample = blocks[b]
        return (
            below + jnp.where(sample < samples, float(BLK), 0.0),
            upto + jnp.where(sample <= samples, float(BLK), 0.0),
        )

    none = jnp.zeros((1, 128), f32)
    low, high = lax.fori_loop(0, n_block, count, (none, none))
    last = lax.broadcasted_iota(jnp.int32, (tok, 128), 1) == 127

    def one_hot(device, hit, always):
        index = device[0]
        for n, i in zip(dims[1:], device[1:]):
            index = index * n + i
        first = index * tok // 128
        skip = pl.multiple_of(lax.rem(index * tok, 128), 32)
        row = jnp.concatenate([pos[pl.ds(first, 1), :], pos[pl.ds(first + 1, 1), :]], axis=1)
        column[...] = as_column(row.astype(f32))
        col = column[pl.ds(skip, tok), :]
        inside = jnp.where((col >= low) & (col < high), hit, 0.0)
        return jnp.where(last, always, inside).astype(bf16)

    def query_hot(s, carry):
        fq[rows_of(s), :] = one_hot(at_z(s // nc, lax.rem(s, nc)), BIG, -BIG)
        return carry

    def key_hot(s, carry):
        fk[rows_of(s), :] = one_hot(at_xy(s // ny, lax.rem(s, ny)), 1.0, 1.0)
        return carry

    lax.fori_loop(0, nk, key_hot, 0)

    lax.fori_loop(0, nq, query_hot, 0)

    xt[:, :, tok:] = jnp.zeros((npc, nzh * chunk, 256 - tok), bf16)
    gr[:, tok:, :] = jnp.zeros((npc, 256 - tok, 384), bf16)
    four = eye(4 * chunk)
    for g in range(nzh * npc // 4):
        turned = dot_nt(four, xb[:, g * 4 * chunk : (g + 1) * 4 * chunk]).astype(bf16)
        for j in range(4):
            n = 4 * g + j
            rows = slice(n // npc * chunk, (n // npc + 1) * chunk)
            xt[n % npc, rows, 0:tok] = turned[j * chunk : (j + 1) * chunk, :]

    def x_block(s, n):
        return send(xt.at[s], xr.at[n], x_send.at[s], x_recv.at[n], at_p(s))

    own = pltpu.make_async_copy(xt.at[me_p], xr.at[me_p], own_sem)
    own.start()

    tq = 256
    score_scale = 1.0 / math.sqrt(128.0)
    rate = score_scale / math.log(2.0)
    def tile(t):
        return pl.ds(pl.multiple_of(t * tq, tq), tq)

    def sweep(moved, block):
        @pl.loop(0, nx * nx)
        def _(t):
            for i in range(nx):

                @pl.when(t == i * i)
                def _():
                    for m in moved:
                        hand_on(m, i)
                    land_k(moved[0], i)

                @pl.when(t == i * i + i)
                def _():
                    for m in moved:
                        land_q(m, i)

            shell = sum(jnp.where(t >= i * i, 1, 0) for i in range(1, nx))
            rest = t - shell * shell
            inner = rest < shell
            ki, qi = jnp.where(inner, shell, rest - shell), jnp.where(inner, rest, shell)
            block(lax.rem(x + near(ki), nx), lax.rem(zh + near(qi), nzh), t)

    def chunk_rows(n, size):
        return pl.ds(pl.multiple_of(n * size, size), size)

    def score_block(kc, qc, t):
        span, at = chunk_rows(kc, key_chunk), chunk_rows(qc, query_chunk)
        query_tile = jnp.concatenate([qb[at, :], fq[at, :]], axis=1)
        s = dot_nt(jnp.concatenate([kb[span, :], fk[span, :]], axis=1), query_tile)
        s_scr[...] = s
        top = jnp.max(s.reshape(key_chunk // 8, 8, query_chunk), axis=0)
        peak = jnp.max(top, axis=0, keepdims=True)
        e = jnp.exp2((s_scr[...] - peak) * rate)
        total = jnp.sum(e.reshape(key_chunk // 8, 8, query_chunk), axis=0)
        et[span, at] = e.astype(bf16)
        pk[kc, :, at] = peak
        lk[kc, :, at] = jnp.sum(total, axis=0, keepdims=True)

    def grad_block(kc, qc, t):
        span, at = chunk_rows(kc, key_chunk), chunk_rows(qc, query_chunk)
        for i in range(nx):

            @pl.when(t == i * i + i)
            def _():
                rows = [db[qc * nzl * nc + n, :, 0:tok] for n in range(nzl * nc)]
                rr[2:3, at] = jnp.concatenate(rows, axis=1)

        @pl.when(t == nx * nx - 3)
        def _():
            for i in range(nzh):
                hand_on(3, i)

        values, turned = vb[span, :], kt[kc]
        for first in range(0, query_chunk, tq):
            wide = min(tq, query_chunk - first)
            part = pl.ds(pl.multiple_of(qc * query_chunk + first, 128), wide)
            slope = dot_nt(values, gb[part, :]) - rr[2:3, part]
            e = et[span, part].astype(f32) * wk[kc, :, part]
            u = (e * slope).astype(bf16)
            et[span, part] = e.astype(bf16)
            ut[span, part] = u
            dqt[:, part] += dot(turned, u)

    sweep((0,), score_block)

    peak = pk[0]
    for n in range(1, nx):
        peak = jnp.maximum(peak, pk[n])
    total = jnp.zeros_like(peak)
    for n in range(nx):
        weight = jnp.exp2((pk[n] - peak) * rate)
        wk[n] = weight
        total = total + lk[n] * weight
    rr[0:1, :] = peak
    rr[1:2, :] = total
    st[me_q] = rr[0:2, :]
    start_q(3)

    def x_block(s, n):
        return send(xt.at[s], xr.at[n], x_send.at[s], x_recv.at[n], at_p(s))

    each(me_p, npc, lambda s: x_block(s, me_p).start())
    for n in range(nx):
        kt[n] = dot_nt(eye(128), kb[n * key_chunk : (n + 1) * key_chunk, :]).astype(bf16)
    dqt[...] = jnp.zeros_like(dqt)
    sweep((1, 2), grad_block)
    for i in range(nzh):
        land_q(3, i)

    peak = st[0, 0:1, :]
    for s in range(1, nq):
        peak = jnp.maximum(peak, st[s, 0:1, :])
    total = jnp.zeros_like(peak)
    for s in range(nq):
        total = total + st[s, 1:2, :] * jnp.exp2((st[s, 0:1, :] - peak) * rate)
    rr[3:4, :] = jnp.exp2((rr[0:1, :] - peak) * rate) / total

    def scale_rows(t):
        at = tile(t)
        factor = rr[3:4, at]
        dqs[at, :] = jnp.transpose(dqt[:, at] * (factor * score_scale)).astype(bf16)
        col = as_column(factor)
        gs[at, :] = (gb[at, :].astype(f32) * col).astype(bf16)
        qs[at, :] = (qb[at, :].astype(f32) * (col * score_scale)).astype(bf16)

    pl.loop(0, n_query // tq)(scale_rows)

    def pair_block(w, core):
        src = dqs.at[rows_of(w * nc + core), :]
        return send(src, dqp.at[w], e_send.at[w], e_recv.at[w], partner)

    def dq_block(w, n):
        return send(dqc.at[w], dqr.at[n], d_send.at[w], d_recv.at[n], at_z(w, c))

    def send_pair(w, carry):
        pair_block(w, other).start()
        return carry

    lax.fori_loop(0, nz, send_pair, 0)

    def send_dq():
        def add(w):
            pair_block(w, c).wait_recv()
            mine = dqs[rows_of(w * nc + c), :].astype(f32)
            dqc[w] = (mine + dqp[w].astype(f32)).astype(bf16)

        def step(w):
            add(w)
            dq_block(w, z).start()

        each_z(step)
        add(z)
        dqr[z] = dqc[z]

    tb = ny * tok

    def kv_block(j, s, n):
        src, dst = ((dks, dkr), (dvs, dvr))[j]
        device = at_xy(s // ny, lax.rem(s, ny))
        return send(src.at[rows_of(s), :], dst.at[n], k_send.at[2 + j, s], k_recv.at[2 + j, n], device)

    def grad_tiles(j, first, end):
        out, left, right = ((dks, ut, qs), (dvs, et, gs))[j]

        def step(i, carry):
            t = lax.rem(x + 2 + i, nx)
            at = pl.ds(pl.multiple_of(t * tb, tb), tb)
            out[at, :] = dot(left[at, :], right[...]).astype(bf16)
            for b in range(ny):
                s = t * ny + b

                @pl.when(s != me_k)
                def _():
                    kv_block(j, s, me_k).start()

            return carry

        lax.fori_loop(first, end, step, 0)

    def summed(ref):
        acc = ref[0].astype(f32)
        for s in range(1, ref.shape[0]):
            acc = acc + ref[s].astype(f32)
        return acc

    def g_block(j, s, device, sem, n):
        ref = gr.at[s, 0:tok, 128 * j : 128 * j + 128]
        return send(ref, ref, sem.at[j, n], p_recv.at[j, s], device)

    def grad_out(j):
        src = gr.at[me_p, 0:tok, 128 * j : 128 * j + 128]
        return pltpu.make_async_copy(src, (dq_out, dk_out, dv_out)[j], out_sem.at[j])

    def send_grad(j, ref):
        gr[me_p, 0:tok, 128 * j : 128 * j + 128] = summed(ref).astype(bf16)
        each_y(lambda b: g_block(j, me_p, (x, zl, zh, b, c), p_send, b).start())
        g_block(j, me_p, partner, h_send, y).start()
        grad_out(j).start()

    def w_block(j, s, n):
        return send(ws.at[j, s], wr.at[j, n], w_send.at[j, s], w_recv.at[j, n], at_zh(s))

    def send_weight(j):
        def land(b):
            s = b * nc + c
            g_block(j, s, partner, h_send, b).wait_recv()
            g_block(j, s, partner, h_send, b).start()

        each_y(land)

        def land_rest(b, carry):
            g_block(j, b * nc + other, partner, h_send, b).wait_recv()
            return carry

        lax.fori_loop(0, ny, land_rest, 0)
        acc = dot(xr[0], gr[0, :, 128 * j : 128 * j + 128])
        for p in range(1, npc):
            acc = acc + dot(xr[p], gr[p, :, 128 * j : 128 * j + 128])
        for n in range(nzh):
            ws[j, n] = acc[n * chunk : (n + 1) * chunk, :].astype(bf16)
        each(zh, nzh, lambda s: w_block(j, s, zh).start())
        wr[j, zh] = ws[j, zh]

    def a_block(j, s, n):
        return send(ar.at[j, n], ar.at[j, n], a_send.at[j, s], a_recv.at[j, n], at_r(s))

    def send_rows(j):
        each(zh, nzh, lambda s: w_block(j, s, s).wait_recv())
        ar[j, me_r] = summed(wr.at[j]).astype(bf16)
        each(me_r, nr, lambda s: a_block(j, s, me_r).start())

    def weight_out(j):
        lanes = slice(128 * j, 128 * j + 128)
        return pltpu.make_async_copy(wg.at[:, lanes], wg_out.at[:, lanes], out_sem.at[3 + j])

    def finish(j):
        each(me_r, nr, lambda s: a_block(j, s, s).wait_recv())
        wg[:, 128 * j : 128 * j + 128] = summed(ar.at[j])
        weight_out(j).start()

    grad_tiles(1, 0, 1)
    send_dq()
    grad_tiles(1, 1, nx)
    dvr[me_k] = dvs[mine_k, :]
    grad_tiles(0, 0, nx)
    dkr[me_k] = dks[mine_k, :]
    each_z(lambda w: dq_block(w, w).wait_recv())
    send_grad(0, dqr)
    own.wait()
    each(me_p, npc, lambda s: x_block(s, s).wait_recv())
    each(me_k, nk, lambda s: kv_block(1, s, s).wait_recv())
    send_grad(2, dvr)
    send_weight(0)
    each(me_k, nk, lambda s: kv_block(0, s, s).wait_recv())
    send_grad(1, dkr)
    send_weight(2)
    send_rows(0)
    send_weight(1)
    send_rows(2)
    finish(0)
    send_rows(1)
    finish(2)
    finish(1)

    for m in range(4):
        each_z(lambda w: q_block(m, me_q, partner, q_send, w).wait_send())

        def f_left(w, carry):
            q_block(m, me_q, partner, f_send, w).wait_send()
            return carry

        lax.fori_loop(0, nz, f_left, 0)

    def pair_left(w, carry):
        pair_block(w, other).wait_send()
        return carry

    lax.fori_loop(0, nz, pair_left, 0)
    each_z(lambda w: dq_block(w, z).wait_send())

    def k_left(s):
        for j in range(2):
            k_block(j, me_k, partner, s).wait_send()
            kv_block(j, s, me_k).wait_send()

    each(me_k, nk, k_left)
    each(me_p, npc, lambda s: x_block(s, me_p).wait_send())

    for j in range(3):
        each_y(lambda b: g_block(j, me_p, partner, p_send, b).wait_send())

        def h_left(b, carry):
            g_block(j, me_p, partner, h_send, b).wait_send()
            return carry

        lax.fori_loop(0, ny, h_left, 0)
        each(zh, nzh, lambda s: w_block(j, s, zh).wait_send())
        each(me_r, nr, lambda s: a_block(j, s, me_r).wait_send())
        grad_out(j).wait()
        weight_out(j).wait()


def hand_out(*refs):
    count = len(refs) // 3
    sources, results, held, sems = refs[:count], refs[count : 2 * count], refs[2 * count : -1], refs[-1]
    into = [pltpu.make_async_copy(sources[i], held[i], sems.at[0, i]) for i in range(count)]
    out = [pltpu.make_async_copy(held[i], results[i], sems.at[1, i]) for i in range(count)]
    for copy in into:
        copy.start()
    for i in range(count):
        into[i].wait()
        out[i].start()
    for copy in out:
        copy.wait()


def local(
    dims, layer_input, queries, key_states, value_states, forward_out, out_grad, token_pos,
    block_sample,
):
    nx, nzl, nzh, ny, nc = dims
    tok = queries.shape[0]
    depth = layer_input.shape[1]
    chunk = depth // (nzh * ny * nc)
    nq, nk, npc, nr = nzh * nzl * nc, nx * ny, ny * nc, nx * nzl
    n_query, n_key = nq * tok, nk * tok
    pos = token_pos.reshape(-1, 128)
    nz = nzh * nzl
    V = pltpu.VMEM
    dma = pltpu.SemaphoreType.DMA
    scratch = [
        V((n_query, 128), bf16), V((n_query, 128), bf16), V((tok, 128), bf16), V((nq, 1, 256), f32),
        V((n_key, 128), bf16), V((n_key, 128), bf16), V((tok, depth), bf16),
        V(pos.shape, jnp.int32), pltpu.SMEM(block_sample.shape, jnp.int32), V((256, 128), f32),
        V((n_query, 128), bf16), V((n_key, 128), bf16), V((nx, 128, ny * tok), bf16),
        V((n_key, n_query), bf16), V((n_key, n_query), bf16), V((ny * tok, nzl * nc * tok), f32),
        V((128, n_query), f32), V((nq, 2, n_query), f32),
        V((nx, 1, n_query), f32), V((nx, 1, n_query), f32), V((nx, 1, n_query), f32), V((8, n_query), f32),
        V((n_query, 128), bf16), V((n_query, 128), bf16),
        V((n_query, 128), bf16), V((nz, tok, 128), bf16), V((nz, tok, 128), bf16),
        V((nz, tok, 128), bf16),
        V((n_key, 128), bf16), V((n_key, 128), bf16),
        V((nk, tok, 128), bf16), V((nk, tok, 128), bf16),
        V((npc, nzh * chunk, 256), bf16), V((npc, nzh * chunk, 256), bf16),
        V((npc, 256, 384), bf16), V((3, nzh, chunk, 128), bf16), V((3, nzh, chunk, 128), bf16),
        V((3, nr, chunk, 128), bf16), V((chunk, 384), f32),
        dma((4, nz)), dma((4, nq)), dma((4, nz)),
        dma((nz,)), dma((nz,)), dma((nz,)), dma((nz,)),
        dma((4, nk)), dma((4, nk)), dma((npc,)), dma((npc,)),
        dma((3, ny)), dma((3, ny)), dma((3, npc)),
        dma((3, nzh)), dma((3, nzh)), dma((3, nr)), dma((3, nr)), dma, dma((8,)), dma((6,)),
    ]

    def body(*refs):
        kernel(dims, *refs)

    hbm = pl.BlockSpec(memory_space=pl.ANY)
    grad = jax.ShapeDtypeStruct((tok, 128), bf16)
    shapes = (grad, grad, grad, jax.ShapeDtypeStruct((chunk, 384), f32))
    results = pl.pallas_call(
        body,
        out_shape=shapes,
        in_specs=[hbm] * 8,
        out_specs=(hbm,) * 4,
        scratch_shapes=scratch,
        compiler_params=pltpu.CompilerParams(
            collective_id=0, has_side_effects=True, vmem_limit_bytes=64 * 2**20
        ),
        name="packed_backward",
    )(queries, key_states, value_states, forward_out, out_grad, layer_input, pos, block_sample)
    return pl.pallas_call(
        hand_out,
        out_shape=shapes,
        in_specs=[hbm] * 4,
        out_specs=(hbm,) * 4,
        scratch_shapes=[V(a.shape, a.dtype) for a in shapes] + [dma((2, 4))],
        name="hand_out",
    )(*results)


def on_mesh(finer):
    dims = tuple(finer.shape[a] for a in AXES)
    slots, cols = P(AXES, None), P(("zh", "y", "c"), None)
    return jax.shard_map(
        lambda *args: local(dims, *args),
        mesh=finer,
        in_specs=(slots,) * 6 + (P(), P()),
        out_specs=(slots, slots, slots, cols),
        check_vma=False,
    )


def solution(mesh):
    return on_mesh(Mesh(mesh.devices.reshape(4, 2, 4, 4, 2), AXES))
```

```python
import math

import jax
import jax.numpy as jnp
from jax import lax
from jax.experimental import pallas as pl
from jax.experimental.pallas import tpu as pltpu
from jax.sharding import Mesh
from jax.sharding import PartitionSpec as P

BLK = 128
BIG = 16384.0
MESH = pl.DeviceIdType.MESH
NT = (((1,), (1,)), ((), ()))
AXES = ("x", "zl", "zh", "y", "c")
bf16 = jnp.bfloat16
f32 = jnp.float32


def dot_nt(a, b, **kw):
    return lax.dot_general(a, b, NT, preferred_element_type=f32, **kw)


def dot(a, b):
    return jnp.dot(a, b, preferred_element_type=f32)


def as_column(row):
    return jnp.transpose(jnp.broadcast_to(row, (128, row.shape[1])))


def eye(n):
    return (
        lax.broadcasted_iota(jnp.int32, (n, n), 0) == lax.broadcasted_iota(jnp.int32, (n, n), 1)
    ).astype(bf16)


def by_distance(n):
    return sorted(range(1, n), key=lambda d: -min(d, n - d))


def near(i):
    return i + i // 2 - 2 * (i // 3)


def kernel(
    dims, q_in, k_in, v_in, o_in, g_in, x_in, pos_ref, block_ref,
    dq_out, dk_out, dv_out, wg_out,
    qb, gb, ob, db, kb, vb, xb, pos, blocks, column, fq, fk, kt, et, ut, s_scr, dqt, st, pk, lk, wk, rr,
    gs, qs,
    dqs, dqp, dqc, dqr, dks, dvs, dkr, dvr, xt, xr, gr, ws, wr, ar, wg,
    q_send, q_recv, f_send, e_send, e_recv, d_send, d_recv, k_send, k_recv,
    x_send, x_recv, p_send, h_send, p_recv, w_send, w_recv, a_send, a_recv, own_sem, in_sem, out_sem,
):
    nx, nzl, nzh, ny, nc = dims
    tok = q_in.shape[0]
    chunk = wg_out.shape[0]
    n_block = block_ref.shape[0]
    x, zl, zh, y, c = (lax.axis_index(a) for a in AXES)
    nz = nzh * nzl
    nq, nk, npc, nr = nz * nc, nx * ny, ny * nc, nx * nzl
    z = zh * nzl + zl
    me_q = z * nc + c
    me_k = x * ny + y
    me_p = y * nc + c
    me_r = x * nzl + zl
    n_query, n_key = nq * tok, nk * tok
    key_chunk, query_chunk = ny * tok, nzl * nc * tok

    def rows_of(s):
        return pl.ds(pl.multiple_of(s * tok, tok), tok)

    def at_z(w, core):
        return (x, lax.rem(w, nzl), w // nzl, y, core)

    def at_xy(a, b):
        return (a, zl, zh, b, c)

    def at_p(s):
        return (x, zl, zh, s // nc, lax.rem(s, nc))

    def at_zh(s):
        return (x, zl, s, y, c)

    def at_r(s):
        return (s // nzl, lax.rem(s, nzl), zh, y, c)

    other = 1 - c
    partner = (x, zl, zh, y, other)

    def send(src, dst, send_sem, recv_sem, device):
        return pltpu.make_async_remote_copy(
            src_ref=src, dst_ref=dst, send_sem=send_sem, recv_sem=recv_sem,
            device_id=device, device_id_type=MESH,
        )

    def each(me, size, body):
        def step(i, carry):
            body(lax.rem(me + i, size))
            return carry

        lax.fori_loop(1, size, step, 0)

    def each_z(body):
        for d in by_distance(nz):
            body(lax.rem(z + d, nz))

    def each_y(body):
        for d in by_distance(ny):
            body(lax.rem(y + d, ny))

    def each_xy(body):
        for i in range(nx):
            for n in range(ny):
                if i or n:
                    body(lax.rem(x + nx - near(i), nx), lax.rem(y + ny - near(n), ny))

    def chunk_z(i, body):
        h = lax.rem(zh + near(i), nzh)
        for n in range(nzl):
            w = h * nzl + n
            if i:
                body(w)
            else:
                pl.when(w != z)(lambda w=w: body(w))

    mine_q, mine_k = rows_of(me_q), rows_of(me_k)
    staged = [
        pltpu.make_async_copy(src, dst, in_sem.at[i])
        for i, (src, dst) in enumerate(
            (
                (k_in, kb.at[mine_k, :]), (q_in, qb.at[mine_q, :]), (v_in, vb.at[mine_k, :]),
                (g_in, gb.at[mine_q, :]), (o_in, ob), (pos_ref, pos), (block_ref, blocks), (x_in, xb),
            )
        )
    ]
    for copy in staged:
        copy.start()

    barrier = pltpu.get_barrier_semaphore()

    def hello(device):
        pl.semaphore_signal(barrier, inc=1, device_id=device, device_id_type=MESH)

    each(me_q, nq, lambda s: hello(at_z(s // nc, lax.rem(s, nc))))
    each(me_k, nk, lambda s: hello(at_xy(s // ny, lax.rem(s, ny))))
    each(me_p, npc, lambda s: hello(at_p(s)))
    each(zh, nzh, lambda s: hello(at_zh(s)))
    each(me_r, nr, lambda s: hello(at_r(s)))

    for copy in staged[:5]:
        copy.wait()
    product = gb[mine_q, :].astype(f32) * ob[...].astype(f32)
    delta = dot_nt(jnp.ones((8, product.shape[1]), f32), product, precision=lax.Precision.HIGHEST)
    db[me_q, :, 0:tok] = delta[0:1, :]
    pl.semaphore_wait(barrier, nq + nk + npc + nzh + nr - 5)

    def q_block(m, s, device, sem, n):
        ref = (qb.at[rows_of(s), :], gb.at[rows_of(s), :], db.at[s], st.at[s])[m]
        return send(ref, ref, sem.at[m, n], q_recv.at[m, s], device)

    def k_block(m, s, device, n):
        ref = (kb, vb)[m].at[rows_of(s), :]
        return send(ref, ref, k_send.at[m, n], k_recv.at[m, s], device)

    def start_q(m):
        for i in range(nzh):
            h = lax.rem(zh + nzh - near(i), nzh)
            for n in range(nzl):
                w = h * nzl + n
                copy = q_block(m, me_q, at_z(w, c), q_send, w)
                if i:
                    copy.start()
                else:
                    pl.when(w != z)(copy.start)
        q_block(m, me_q, partner, f_send, z).start()

    def start_k(m):
        each_xy(lambda a, b: k_block(m, me_k, at_xy(a, b), a * ny + b).start())

    def hand_on(m, i):
        def land(w):
            s = w * nc + c
            q_block(m, s, partner, f_send, w).wait_recv()
            q_block(m, s, partner, f_send, w).start()

        chunk_z(i, land)

    def land_q(m, i):
        h = lax.rem(zh + near(i), nzh)
        for n in range(nzl):
            w = h * nzl + n
            q_block(m, w * nc + other, partner, f_send, w).wait_recv()

    def land_k(m, i):
        a = lax.rem(x + near(i), nx)
        for n in range(ny):
            if i or n:
                s = a * ny + lax.rem(y + near(n), ny)
                k_block(m, s, partner, s).wait_recv()

    start_q(0)
    start_k(0)

    for copy in staged[5:]:
        copy.wait()
    samples = lax.broadcasted_iota(jnp.int32, (1, 128), 1)

    def count(b, carry):
        below, upto = carry
        sample = blocks[b]
        return (
            below + jnp.where(sample < samples, float(BLK), 0.0),
            upto + jnp.where(sample <= samples, float(BLK), 0.0),
        )

    none = jnp.zeros((1, 128), f32)
    low, high = lax.fori_loop(0, n_block, count, (none, none))
    last = lax.broadcasted_iota(jnp.int32, (tok, 128), 1) == 127

    def one_hot(device, hit, always):
        index = device[0]
        for n, i in zip(dims[1:], device[1:]):
            index = index * n + i
        first = index * tok // 128
        skip = pl.multiple_of(lax.rem(index * tok, 128), 32)
        row = jnp.concatenate([pos[pl.ds(first, 1), :], pos[pl.ds(first + 1, 1), :]], axis=1)
        column[...] = as_column(row.astype(f32))
        col = column[pl.ds(skip, tok), :]
        inside = jnp.where((col >= low) & (col < high), hit, 0.0)
        return jnp.where(last, always, inside).astype(bf16)

    def query_hot(s, carry):
        fq[rows_of(s), :] = one_hot(at_z(s // nc, lax.rem(s, nc)), BIG, -BIG)
        return carry

    def key_hot(s, carry):
        fk[rows_of(s), :] = one_hot(at_xy(s // ny, lax.rem(s, ny)), 1.0, 1.0)
        return carry

    lax.fori_loop(0, nk, key_hot, 0)

    lax.fori_loop(0, nq, query_hot, 0)

    xt[:, :, tok:] = jnp.zeros((npc, nzh * chunk, 256 - tok), bf16)
    gr[:, tok:, :] = jnp.zeros((npc, 256 - tok, 384), bf16)
    four = eye(4 * chunk)
    for g in range(nzh * npc // 4):
        turned = dot_nt(four, xb[:, g * 4 * chunk : (g + 1) * 4 * chunk]).astype(bf16)
        for j in range(4):
            n = 4 * g + j
            rows = slice(n // npc * chunk, (n // npc + 1) * chunk)
            xt[n % npc, rows, 0:tok] = turned[j * chunk : (j + 1) * chunk, :]

    def x_block(s, n):
        return send(xt.at[s], xr.at[n], x_send.at[s], x_recv.at[n], at_p(s))

    own = pltpu.make_async_copy(xt.at[me_p], xr.at[me_p], own_sem)
    own.start()

    tq = 256
    score_scale = 1.0 / math.sqrt(128.0)
    rate = score_scale / math.log(2.0)
    def tile(t):
        return pl.ds(pl.multiple_of(t * tq, tq), tq)

    def sweep(moved, block):
        @pl.loop(0, nx * nx)
        def _(t):
            for i in range(nx):

                @pl.when(t == i * i)
                def _():
                    for m in moved:
                        hand_on(m, i)
                    land_k(moved[0], i)

                @pl.when(t == i * i + i)
                def _():
                    for m in moved:
                        land_q(m, i)

            shell = sum(jnp.where(t >= i * i, 1, 0) for i in range(1, nx))
            rest = t - shell * shell
            inner = rest < shell
            ki, qi = jnp.where(inner, shell, rest - shell), jnp.where(inner, rest, shell)
            block(lax.rem(x + near(ki), nx), lax.rem(zh + near(qi), nzh), t)

    def chunk_rows(n, size):
        return pl.ds(pl.multiple_of(n * size, size), size)

    def score_block(kc, qc, t):
        @pl.when(t == min(3, nx * nx - 1))
        def _():
            start_q(2)
            start_q(1)
            start_k(1)

        span, at = chunk_rows(kc, key_chunk), chunk_rows(qc, query_chunk)
        query_tile = jnp.concatenate([qb[at, :], fq[at, :]], axis=1)
        s = dot_nt(jnp.concatenate([kb[span, :], fk[span, :]], axis=1), query_tile)
        s_scr[...] = s
        top = jnp.max(s.reshape(key_chunk // 8, 8, query_chunk), axis=0)
        peak = jnp.max(top, axis=0, keepdims=True)
        e = jnp.exp2((s_scr[...] - peak) * rate)
        total = jnp.sum(e.reshape(key_chunk // 8, 8, query_chunk), axis=0)
        et[span, at] = e.astype(bf16)
        pk[kc, :, at] = peak
        lk[kc, :, at] = jnp.sum(total, axis=0, keepdims=True)

    def grad_block(kc, qc, t):
        span, at = chunk_rows(kc, key_chunk), chunk_rows(qc, query_chunk)
        for i in range(nx):

            @pl.when(t == i * i + i)
            def _():
                rows = [db[qc * nzl * nc + n, :, 0:tok] for n in range(nzl * nc)]
                rr[2:3, at] = jnp.concatenate(rows, axis=1)

        @pl.when(t == nx * nx - 3)
        def _():
            for i in range(nzh):
                hand_on(3, i)

        values = vb[span, :]
        for first in range(0, query_chunk, tq):
            wide = min(tq, query_chunk - first)
            part = pl.ds(pl.multiple_of(qc * query_chunk + first, 128), wide)
            slope = dot_nt(values, gb[part, :]) - rr[2:3, part]
            e = et[span, part].astype(f32) * wk[kc, :, part]
            u = (e * slope).astype(bf16)
            et[span, part] = e.astype(bf16)
            ut[span, part] = u

    sweep((0,), score_block)

    peak = pk[0]
    for n in range(1, nx):
        peak = jnp.maximum(peak, pk[n])
    total = jnp.zeros_like(peak)
    for n in range(nx):
        weight = jnp.exp2((pk[n] - peak) * rate)
        wk[n] = weight
        total = total + lk[n] * weight
    rr[0:1, :] = peak
    rr[1:2, :] = total
    st[me_q] = rr[0:2, :]
    start_q(3)

    def x_block(s, n):
        return send(xt.at[s], xr.at[n], x_send.at[s], x_recv.at[n], at_p(s))

    each(me_p, npc, lambda s: x_block(s, me_p).start())
    kt[...] = dot_nt(eye(128), kb[...]).astype(bf16)
    sweep((1, 2), grad_block)
    wide = 512 if n_query % 512 == 0 else tq

    @pl.loop(0, n_query // wide)
    def _(t):
        at = pl.ds(pl.multiple_of(t * wide, wide), wide)
        dqt[:, at] = dot(kt[...], ut[:, at])

    for i in range(nzh):
        land_q(3, i)

    peak = st[0, 0:1, :]
    for s in range(1, nq):
        peak = jnp.maximum(peak, st[s, 0:1, :])
    total = jnp.zeros_like(peak)
    for s in range(nq):
        total = total + st[s, 1:2, :] * jnp.exp2((st[s, 0:1, :] - peak) * rate)
    rr[3:4, :] = jnp.exp2((rr[0:1, :] - peak) * rate) / total

    def scale_rows(t):
        at = tile(t)
        factor = rr[3:4, at]
        dqs[at, :] = jnp.transpose(dqt[:, at] * (factor * score_scale)).astype(bf16)
        col = as_column(factor)
        gs[at, :] = (gb[at, :].astype(f32) * col).astype(bf16)
        qs[at, :] = (qb[at, :].astype(f32) * (col * score_scale)).astype(bf16)

    pl.loop(0, n_query // tq)(scale_rows)

    def pair_block(w, core):
        src = dqs.at[rows_of(w * nc + core), :]
        return send(src, dqp.at[w], e_send.at[w], e_recv.at[w], partner)

    def dq_block(w, n):
        return send(dqc.at[w], dqr.at[n], d_send.at[w], d_recv.at[n], at_z(w, c))

    def send_pair(w, carry):
        pair_block(w, other).start()
        return carry

    lax.fori_loop(0, nz, send_pair, 0)

    def send_dq():
        def add(w):
            pair_block(w, c).wait_recv()
            mine = dqs[rows_of(w * nc + c), :].astype(f32)
            dqc[w] = (mine + dqp[w].astype(f32)).astype(bf16)

        def step(w):
            add(w)
            dq_block(w, z).start()

        each_z(step)
        add(z)
        dqr[z] = dqc[z]

    tb = ny * tok

    def kv_block(j, s, n):
        src, dst = ((dks, dkr), (dvs, dvr))[j]
        device = at_xy(s // ny, lax.rem(s, ny))
        return send(src.at[rows_of(s), :], dst.at[n], k_send.at[2 + j, s], k_recv.at[2 + j, n], device)

    def grad_tiles(j, first, end):
        out, left, right = ((dks, ut, qs), (dvs, et, gs))[j]

        def step(i, carry):
            t = lax.rem(x + 2 + i, nx)
            at = pl.ds(pl.multiple_of(t * tb, tb), tb)
            out[at, :] = dot(left[at, :], right[...]).astype(bf16)
            for b in range(ny):
                s = t * ny + b

                @pl.when(s != me_k)
                def _():
                    kv_block(j, s, me_k).start()

            return carry

        lax.fori_loop(first, end, step, 0)

    def summed(ref):
        acc = ref[0].astype(f32)
        for s in range(1, ref.shape[0]):
            acc = acc + ref[s].astype(f32)
        return acc

    def g_block(j, s, device, sem, n):
        ref = gr.at[s, 0:tok, 128 * j : 128 * j + 128]
        return send(ref, ref, sem.at[j, n], p_recv.at[j, s], device)

    def grad_out(j):
        src = gr.at[me_p, 0:tok, 128 * j : 128 * j + 128]
        return pltpu.make_async_copy(src, (dq_out, dk_out, dv_out)[j], out_sem.at[j])

    def send_grad(j, ref):
        gr[me_p, 0:tok, 128 * j : 128 * j + 128] = summed(ref).astype(bf16)
        each_y(lambda b: g_block(j, me_p, (x, zl, zh, b, c), p_send, b).start())
        g_block(j, me_p, partner, h_send, y).start()
        grad_out(j).start()

    def w_block(j, s, n):
        return send(ws.at[j, s], wr.at[j, n], w_send.at[j, s], w_recv.at[j, n], at_zh(s))

    def send_weight(j):
        def land(b):
            s = b * nc + c
            g_block(j, s, partner, h_send, b).wait_recv()
            g_block(j, s, partner, h_send, b).start()

        each_y(land)

        def land_rest(b, carry):
            g_block(j, b * nc + other, partner, h_send, b).wait_recv()
            return carry

        lax.fori_loop(0, ny, land_rest, 0)
        acc = dot(xr[0], gr[0, :, 128 * j : 128 * j + 128])
        for p in range(1, npc):
            acc = acc + dot(xr[p], gr[p, :, 128 * j : 128 * j + 128])
        for n in range(nzh):
            ws[j, n] = acc[n * chunk : (n + 1) * chunk, :].astype(bf16)
        each(zh, nzh, lambda s: w_block(j, s, zh).start())
        wr[j, zh] = ws[j, zh]

    def a_block(j, s, n):
        return send(ar.at[j, n], ar.at[j, n], a_send.at[j, s], a_recv.at[j, n], at_r(s))

    def send_rows(j):
        each(zh, nzh, lambda s: w_block(j, s, s).wait_recv())
        ar[j, me_r] = summed(wr.at[j]).astype(bf16)
        each(me_r, nr, lambda s: a_block(j, s, me_r).start())

    def weight_out(j):
        lanes = slice(128 * j, 128 * j + 128)
        return pltpu.make_async_copy(wg.at[:, lanes], wg_out.at[:, lanes], out_sem.at[3 + j])

    def finish(j):
        each(me_r, nr, lambda s: a_block(j, s, s).wait_recv())
        wg[:, 128 * j : 128 * j + 128] = summed(ar.at[j])
        weight_out(j).start()

    grad_tiles(1, 0, 1)
    send_dq()
    grad_tiles(1, 1, nx)
    dvr[me_k] = dvs[mine_k, :]
    grad_tiles(0, 0, nx)
    dkr[me_k] = dks[mine_k, :]
    each_z(lambda w: dq_block(w, w).wait_recv())
    send_grad(0, dqr)
    own.wait()
    each(me_p, npc, lambda s: x_block(s, s).wait_recv())
    each(me_k, nk, lambda s: kv_block(1, s, s).wait_recv())
    send_grad(2, dvr)
    send_weight(0)
    each(me_k, nk, lambda s: kv_block(0, s, s).wait_recv())
    send_grad(1, dkr)
    send_weight(2)
    send_rows(0)
    send_weight(1)
    send_rows(2)
    finish(0)
    send_rows(1)
    finish(2)
    finish(1)

    for m in range(4):
        each_z(lambda w: q_block(m, me_q, partner, q_send, w).wait_send())

        def f_left(w, carry):
            q_block(m, me_q, partner, f_send, w).wait_send()
            return carry

        lax.fori_loop(0, nz, f_left, 0)

    def pair_left(w, carry):
        pair_block(w, other).wait_send()
        return carry

    lax.fori_loop(0, nz, pair_left, 0)
    each_z(lambda w: dq_block(w, z).wait_send())

    def k_left(s):
        for j in range(2):
            k_block(j, me_k, partner, s).wait_send()
            kv_block(j, s, me_k).wait_send()

    each(me_k, nk, k_left)
    each(me_p, npc, lambda s: x_block(s, me_p).wait_send())

    for j in range(3):
        each_y(lambda b: g_block(j, me_p, partner, p_send, b).wait_send())

        def h_left(b, carry):
            g_block(j, me_p, partner, h_send, b).wait_send()
            return carry

        lax.fori_loop(0, ny, h_left, 0)
        each(zh, nzh, lambda s: w_block(j, s, zh).wait_send())
        each(me_r, nr, lambda s: a_block(j, s, me_r).wait_send())
        grad_out(j).wait()
        weight_out(j).wait()


def hand_out(*refs):
    count = len(refs) // 3
    sources, results, held, sems = refs[:count], refs[count : 2 * count], refs[2 * count : -1], refs[-1]
    into = [pltpu.make_async_copy(sources[i], held[i], sems.at[0, i]) for i in range(count)]
    out = [pltpu.make_async_copy(held[i], results[i], sems.at[1, i]) for i in range(count)]
    for copy in into:
        copy.start()
    for i in range(count):
        into[i].wait()
        out[i].start()
    for copy in out:
        copy.wait()


def local(
    dims, layer_input, queries, key_states, value_states, forward_out, out_grad, token_pos,
    block_sample,
):
    nx, nzl, nzh, ny, nc = dims
    tok = queries.shape[0]
    depth = layer_input.shape[1]
    chunk = depth // (nzh * ny * nc)
    nq, nk, npc, nr = nzh * nzl * nc, nx * ny, ny * nc, nx * nzl
    n_query, n_key = nq * tok, nk * tok
    pos = token_pos.reshape(-1, 128)
    nz = nzh * nzl
    V = pltpu.VMEM
    dma = pltpu.SemaphoreType.DMA
    scratch = [
        V((n_query, 128), bf16), V((n_query, 128), bf16), V((tok, 128), bf16), V((nq, 1, 256), f32),
        V((n_key, 128), bf16), V((n_key, 128), bf16), V((tok, depth), bf16),
        V(pos.shape, jnp.int32), pltpu.SMEM(block_sample.shape, jnp.int32), V((256, 128), f32),
        V((n_query, 128), bf16), V((n_key, 128), bf16), V((128, n_key), bf16),
        V((n_key, n_query), bf16), V((n_key, n_query), bf16), V((ny * tok, nzl * nc * tok), f32),
        V((128, n_query), f32), V((nq, 2, n_query), f32),
        V((nx, 1, n_query), f32), V((nx, 1, n_query), f32), V((nx, 1, n_query), f32), V((8, n_query), f32),
        V((n_query, 128), bf16), V((n_query, 128), bf16),
        V((n_query, 128), bf16), V((nz, tok, 128), bf16), V((nz, tok, 128), bf16),
        V((nz, tok, 128), bf16),
        V((n_key, 128), bf16), V((n_key, 128), bf16),
        V((nk, tok, 128), bf16), V((nk, tok, 128), bf16),
        V((npc, nzh * chunk, 256), bf16), V((npc, nzh * chunk, 256), bf16),
        V((npc, 256, 384), bf16), V((3, nzh, chunk, 128), bf16), V((3, nzh, chunk, 128), bf16),
        V((3, nr, chunk, 128), bf16), V((chunk, 384), f32),
        dma((4, nz)), dma((4, nq)), dma((4, nz)),
        dma((nz,)), dma((nz,)), dma((nz,)), dma((nz,)),
        dma((4, nk)), dma((4, nk)), dma((npc,)), dma((npc,)),
        dma((3, ny)), dma((3, ny)), dma((3, npc)),
        dma((3, nzh)), dma((3, nzh)), dma((3, nr)), dma((3, nr)), dma, dma((8,)), dma((6,)),
    ]

    def body(*refs):
        kernel(dims, *refs)

    hbm = pl.BlockSpec(memory_space=pl.ANY)
    grad = jax.ShapeDtypeStruct((tok, 128), bf16)
    shapes = (grad, grad, grad, jax.ShapeDtypeStruct((chunk, 384), f32))
    results = pl.pallas_call(
        body,
        out_shape=shapes,
        in_specs=[hbm] * 8,
        out_specs=(hbm,) * 4,
        scratch_shapes=scratch,
        compiler_params=pltpu.CompilerParams(
            collective_id=0, has_side_effects=True, vmem_limit_bytes=64 * 2**20
        ),
        name="packed_backward",
    )(queries, key_states, value_states, forward_out, out_grad, layer_input, pos, block_sample)
    return pl.pallas_call(
        hand_out,
        out_shape=shapes,
        in_specs=[hbm] * 4,
        out_specs=(hbm,) * 4,
        scratch_shapes=[V(a.shape, a.dtype) for a in shapes] + [dma((2, 4))],
        name="hand_out",
    )(*results)


def on_mesh(finer):
    dims = tuple(finer.shape[a] for a in AXES)
    slots, cols = P(AXES, None), P(("zh", "y", "c"), None)
    return jax.shard_map(
        lambda *args: local(dims, *args),
        mesh=finer,
        in_specs=(slots,) * 6 + (P(), P()),
        out_specs=(slots, slots, slots, cols),
        check_vma=False,
    )


def solution(mesh):
    return on_mesh(Mesh(mesh.devices.reshape(4, 2, 4, 4, 2), AXES))
```

```python
import math

import jax
import jax.numpy as jnp
from jax import lax
from jax.experimental import pallas as pl
from jax.experimental.pallas import tpu as pltpu
from jax.sharding import Mesh
from jax.sharding import PartitionSpec as P

BLK = 128
BIG = 16384.0
MESH = pl.DeviceIdType.MESH
NT = (((1,), (1,)), ((), ()))
AXES = ("x", "zl", "zh", "y", "c")
bf16 = jnp.bfloat16
f32 = jnp.float32


def dot_nt(a, b, **kw):
    return lax.dot_general(a, b, NT, preferred_element_type=f32, **kw)


def dot(a, b):
    return jnp.dot(a, b, preferred_element_type=f32)


def as_column(row):
    return jnp.transpose(jnp.broadcast_to(row, (128, row.shape[1])))


def eye(n):
    return (
        lax.broadcasted_iota(jnp.int32, (n, n), 0) == lax.broadcasted_iota(jnp.int32, (n, n), 1)
    ).astype(bf16)


def by_distance(n):
    return sorted(range(1, n), key=lambda d: -min(d, n - d))


def near(i):
    return i + i // 2 - 2 * (i // 3)


def kernel(
    dims, q_in, k_in, v_in, o_in, g_in, x_in, pos_ref, block_ref,
    dq_out, dk_out, dv_out, wg_out,
    qb, gb, ob, db, kb, vb, xb, pos, blocks, column, fq, fk, kt, et, ut, s_scr, dqt, st, pk, lk, wk, rr,
    gs, qs,
    dqs, dqp, dqc, dqr, dks, dvs, dkr, dvr, xt, xr, gr, ws, wr, ar, wg,
    q_send, q_recv, f_send, e_send, e_recv, d_send, d_recv, k_send, k_recv,
    x_send, x_recv, p_send, h_send, p_recv, w_send, w_recv, a_send, a_recv, own_sem, in_sem, out_sem,
):
    nx, nzl, nzh, ny, nc = dims
    tok = q_in.shape[0]
    chunk = wg_out.shape[0]
    n_block = block_ref.shape[0]
    x, zl, zh, y, c = (lax.axis_index(a) for a in AXES)
    nz = nzh * nzl
    nq, nk, npc, nr = nz * nc, nx * ny, ny * nc, nx * nzl
    z = zh * nzl + zl
    me_q = z * nc + c
    me_k = x * ny + y
    me_p = y * nc + c
    me_r = x * nzl + zl
    n_query, n_key = nq * tok, nk * tok
    key_chunk, query_chunk = ny * tok, nzl * nc * tok

    def rows_of(s):
        return pl.ds(pl.multiple_of(s * tok, tok), tok)

    def at_z(w, core):
        return (x, lax.rem(w, nzl), w // nzl, y, core)

    def at_xy(a, b):
        return (a, zl, zh, b, c)

    def at_p(s):
        return (x, zl, zh, s // nc, lax.rem(s, nc))

    def at_zh(s):
        return (x, zl, s, y, c)

    def at_r(s):
        return (s // nzl, lax.rem(s, nzl), zh, y, c)

    other = 1 - c
    partner = (x, zl, zh, y, other)

    def send(src, dst, send_sem, recv_sem, device):
        return pltpu.make_async_remote_copy(
            src_ref=src, dst_ref=dst, send_sem=send_sem, recv_sem=recv_sem,
            device_id=device, device_id_type=MESH,
        )

    def each(me, size, body):
        def step(i, carry):
            body(lax.rem(me + i, size))
            return carry

        lax.fori_loop(1, size, step, 0)

    def each_z(body):
        for d in by_distance(nz):
            body(lax.rem(z + d, nz))

    def each_y(body):
        for d in by_distance(ny):
            body(lax.rem(y + d, ny))

    def each_xy(body):
        for i in range(nx):
            for n in range(ny):
                if i or n:
                    body(lax.rem(x + nx - near(i), nx), lax.rem(y + ny - near(n), ny))

    def chunk_z(i, body):
        h = lax.rem(zh + near(i), nzh)
        for n in range(nzl):
            w = h * nzl + n
            if i:
                body(w)
            else:
                pl.when(w != z)(lambda w=w: body(w))

    mine_q, mine_k = rows_of(me_q), rows_of(me_k)
    staged = [
        pltpu.make_async_copy(src, dst, in_sem.at[i])
        for i, (src, dst) in enumerate(
            (
                (k_in, kb.at[mine_k, :]), (q_in, qb.at[mine_q, :]), (v_in, vb.at[mine_k, :]),
                (g_in, gb.at[mine_q, :]), (o_in, ob), (pos_ref, pos), (block_ref, blocks), (x_in, xb),
            )
        )
    ]
    for copy in staged:
        copy.start()

    barrier = pltpu.get_barrier_semaphore()

    def hello(device):
        pl.semaphore_signal(barrier, inc=1, device_id=device, device_id_type=MESH)

    each(me_q, nq, lambda s: hello(at_z(s // nc, lax.rem(s, nc))))
    each(me_k, nk, lambda s: hello(at_xy(s // ny, lax.rem(s, ny))))
    each(me_p, npc, lambda s: hello(at_p(s)))
    each(zh, nzh, lambda s: hello(at_zh(s)))
    each(me_r, nr, lambda s: hello(at_r(s)))

    for copy in staged[:5]:
        copy.wait()
    product = gb[mine_q, :].astype(f32) * ob[...].astype(f32)
    delta = dot_nt(jnp.ones((8, product.shape[1]), f32), product, precision=lax.Precision.HIGHEST)
    db[me_q, :, 0:tok] = delta[0:1, :]
    pl.semaphore_wait(barrier, nq + nk + npc + nzh + nr - 5)

    def q_block(m, s, device, sem, n):
        ref = (qb.at[rows_of(s), :], gb.at[rows_of(s), :], db.at[s], st.at[s])[m]
        return send(ref, ref, sem.at[m, n], q_recv.at[m, s], device)

    def k_block(m, s, device, n):
        ref = (kb, vb)[m].at[rows_of(s), :]
        return send(ref, ref, k_send.at[m, n], k_recv.at[m, s], device)

    def start_q(m):
        for i in range(nzh):
            h = lax.rem(zh + nzh - near(i), nzh)
            for n in range(nzl):
                w = h * nzl + n
                copy = q_block(m, me_q, at_z(w, c), q_send, w)
                if i:
                    copy.start()
                else:
                    pl.when(w != z)(copy.start)
        q_block(m, me_q, partner, f_send, z).start()

    def start_k(m):
        each_xy(lambda a, b: k_block(m, me_k, at_xy(a, b), a * ny + b).start())

    def hand_on(m, i):
        def land(w):
            s = w * nc + c
            q_block(m, s, partner, f_send, w).wait_recv()
            q_block(m, s, partner, f_send, w).start()

        chunk_z(i, land)

    def land_q(m, i):
        h = lax.rem(zh + near(i), nzh)
        for n in range(nzl):
            w = h * nzl + n
            q_block(m, w * nc + other, partner, f_send, w).wait_recv()

    def land_k(m, i):
        a = lax.rem(x + near(i), nx)
        for n in range(ny):
            if i or n:
                s = a * ny + lax.rem(y + near(n), ny)
                k_block(m, s, partner, s).wait_recv()

    start_q(0)
    start_k(0)

    for copy in staged[5:]:
        copy.wait()
    samples = lax.broadcasted_iota(jnp.int32, (1, 128), 1)

    def count(b, carry):
        below, upto = carry
        sample = blocks[b]
        return (
            below + jnp.where(sample < samples, float(BLK), 0.0),
            upto + jnp.where(sample <= samples, float(BLK), 0.0),
        )

    none = jnp.zeros((1, 128), f32)
    low, high = lax.fori_loop(0, n_block, count, (none, none))
    last = lax.broadcasted_iota(jnp.int32, (tok, 128), 1) == 127

    def one_hot(device, hit, always):
        index = device[0]
        for n, i in zip(dims[1:], device[1:]):
            index = index * n + i
        first = index * tok // 128
        skip = pl.multiple_of(lax.rem(index * tok, 128), 32)
        row = jnp.concatenate([pos[pl.ds(first, 1), :], pos[pl.ds(first + 1, 1), :]], axis=1)
        column[...] = as_column(row.astype(f32))
        col = column[pl.ds(skip, tok), :]
        inside = jnp.where((col >= low) & (col < high), hit, 0.0)
        return jnp.where(last, always, inside).astype(bf16)

    def query_hot(s, carry):
        fq[rows_of(s), :] = one_hot(at_z(s // nc, lax.rem(s, nc)), BIG, -BIG)
        return carry

    def key_hot(s, carry):
        fk[rows_of(s), :] = one_hot(at_xy(s // ny, lax.rem(s, ny)), 1.0, 1.0)
        return carry

    lax.fori_loop(0, nk, key_hot, 0)

    lax.fori_loop(0, nq, query_hot, 0)

    tq = 256
    score_scale = 1.0 / math.sqrt(128.0)
    rate = score_scale / math.log(2.0)
    def tile(t):
        return pl.ds(pl.multiple_of(t * tq, tq), tq)

    def sweep(moved, block):
        @pl.loop(0, nx * nx)
        def _(t):
            for i in range(nx):

                @pl.when(t == i * i)
                def _():
                    for m in moved:
                        hand_on(m, i)
                    land_k(moved[0], i)

                @pl.when(t == i * i + i)
                def _():
                    for m in moved:
                        land_q(m, i)

            shell = sum(jnp.where(t >= i * i, 1, 0) for i in range(1, nx))
            rest = t - shell * shell
            inner = rest < shell
            ki, qi = jnp.where(inner, shell, rest - shell), jnp.where(inner, rest, shell)
            block(lax.rem(x + near(ki), nx), lax.rem(zh + near(qi), nzh), t)

    def chunk_rows(n, size):
        return pl.ds(pl.multiple_of(n * size, size), size)

    def score_block(kc, qc, t):
        @pl.when(t == 1)
        def _():
            start_q(2)
            start_q(1)
            start_k(1)

        span, at = chunk_rows(kc, key_chunk), chunk_rows(qc, query_chunk)
        query_tile = jnp.concatenate([qb[at, :], fq[at, :]], axis=1)
        s = dot_nt(jnp.concatenate([kb[span, :], fk[span, :]], axis=1), query_tile)
        s_scr[...] = s
        top = jnp.max(s.reshape(key_chunk // 8, 8, query_chunk), axis=0)
        peak = jnp.max(top, axis=0, keepdims=True)
        e = jnp.exp2((s_scr[...] - peak) * rate)
        total = jnp.sum(e.reshape(key_chunk // 8, 8, query_chunk), axis=0)
        et[span, at] = e.astype(bf16)
        pk[kc, :, at] = peak
        lk[kc, :, at] = jnp.sum(total, axis=0, keepdims=True)

    def grad_block(kc, qc, t):
        span, at = chunk_rows(kc, key_chunk), chunk_rows(qc, query_chunk)
        for i in range(nx):

            @pl.when(t == i * i + i)
            def _():
                rows = [db[qc * nzl * nc + n, :, 0:tok] for n in range(nzl * nc)]
                rr[2:3, at] = jnp.concatenate(rows, axis=1)

        @pl.when(t == nx * nx - 3)
        def _():
            for i in range(nzh):
                hand_on(3, i)

        values = vb[span, :]
        for first in range(0, query_chunk, tq):
            wide = min(tq, query_chunk - first)
            part = pl.ds(pl.multiple_of(qc * query_chunk + first, 128), wide)
            slope = dot_nt(values, gb[part, :]) - rr[2:3, part]
            e = et[span, part].astype(f32) * wk[kc, :, part]
            u = (e * slope).astype(bf16)
            et[span, part] = e.astype(bf16)
            ut[span, part] = u

    sweep((0,), score_block)

    peak = pk[0]
    for n in range(1, nx):
        peak = jnp.maximum(peak, pk[n])
    total = jnp.zeros_like(peak)
    for n in range(nx):
        weight = jnp.exp2((pk[n] - peak) * rate)
        wk[n] = weight
        total = total + lk[n] * weight
    rr[0:1, :] = peak
    rr[1:2, :] = total
    st[me_q] = rr[0:2, :]
    start_q(3)

    xt[:, :, tok:] = jnp.zeros((npc, nzh * chunk, 256 - tok), bf16)
    gr[:, tok:, :] = jnp.zeros((npc, 256 - tok, 384), bf16)
    four = eye(4 * chunk)
    for g in range(nzh * npc // 4):
        turned = dot_nt(four, xb[:, g * 4 * chunk : (g + 1) * 4 * chunk]).astype(bf16)
        for j in range(4):
            n = 4 * g + j
            rows = slice(n // npc * chunk, (n // npc + 1) * chunk)
            xt[n % npc, rows, 0:tok] = turned[j * chunk : (j + 1) * chunk, :]

    def x_block(s, n):
        return send(xt.at[s], xr.at[n], x_send.at[s], x_recv.at[n], at_p(s))

    own = pltpu.make_async_copy(xt.at[me_p], xr.at[me_p], own_sem)
    own.start()

    def x_block(s, n):
        return send(xt.at[s], xr.at[n], x_send.at[s], x_recv.at[n], at_p(s))

    each(me_p, npc, lambda s: x_block(s, me_p).start())
    kt[...] = dot_nt(eye(128), kb[...]).astype(bf16)
    sweep((1, 2), grad_block)
    for i in range(nzh):
        land_q(3, i)

    peak = st[0, 0:1, :]
    for s in range(1, nq):
        peak = jnp.maximum(peak, st[s, 0:1, :])
    total = jnp.zeros_like(peak)
    for s in range(nq):
        total = total + st[s, 1:2, :] * jnp.exp2((st[s, 0:1, :] - peak) * rate)
    rr[3:4, :] = jnp.exp2((rr[0:1, :] - peak) * rate) / total

    @pl.loop(0, n_query // tq)
    def _(t):
        at = tile(t)
        gs[at, :] = (gb[at, :].astype(f32) * as_column(rr[3:4, at])).astype(bf16)

    def query_grads():
        wide = 512 if n_query % 512 == 0 else tq

        @pl.loop(0, n_query // wide)
        def _(t):
            at = pl.ds(pl.multiple_of(t * wide, wide), wide)
            dqt[:, at] = dot(kt[...], ut[:, at])

        @pl.loop(0, n_query // tq)
        def _(t):
            at = tile(t)
            factor = rr[3:4, at] * score_scale
            dqs[at, :] = jnp.transpose(dqt[:, at] * factor).astype(bf16)
            qs[at, :] = (qb[at, :].astype(f32) * as_column(factor)).astype(bf16)

    def pair_block(w, core):
        src = dqs.at[rows_of(w * nc + core), :]
        return send(src, dqp.at[w], e_send.at[w], e_recv.at[w], partner)

    def dq_block(w, n):
        return send(dqc.at[w], dqr.at[n], d_send.at[w], d_recv.at[n], at_z(w, c))

    def send_pair(w, carry):
        pair_block(w, other).start()
        return carry

    def send_dq():
        def add(w):
            pair_block(w, c).wait_recv()
            mine = dqs[rows_of(w * nc + c), :].astype(f32)
            dqc[w] = (mine + dqp[w].astype(f32)).astype(bf16)

        def step(w):
            add(w)
            dq_block(w, z).start()

        each_z(step)
        add(z)
        dqr[z] = dqc[z]

    tb = ny * tok

    def kv_block(j, s, n):
        src, dst = ((dks, dkr), (dvs, dvr))[j]
        device = at_xy(s // ny, lax.rem(s, ny))
        return send(src.at[rows_of(s), :], dst.at[n], k_send.at[2 + j, s], k_recv.at[2 + j, n], device)

    def grad_tiles(j, first, end):
        out, left, right = ((dks, ut, qs), (dvs, et, gs))[j]

        def step(i, carry):
            last = nx - 1 - i
            t = lax.rem(x + last + last // 2 - 2 * (last // 3), nx)
            at = pl.ds(pl.multiple_of(t * tb, tb), tb)
            out[at, :] = dot(left[at, :], right[...]).astype(bf16)
            for b in range(ny):
                s = t * ny + b

                @pl.when(s != me_k)
                def _():
                    kv_block(j, s, me_k).start()

            return carry

        lax.fori_loop(first, end, step, 0)

    def summed(ref):
        acc = ref[0].astype(f32)
        for s in range(1, ref.shape[0]):
            acc = acc + ref[s].astype(f32)
        return acc

    def g_block(j, s, device, sem, n):
        ref = gr.at[s, 0:tok, 128 * j : 128 * j + 128]
        return send(ref, ref, sem.at[j, n], p_recv.at[j, s], device)

    def grad_out(j):
        src = gr.at[me_p, 0:tok, 128 * j : 128 * j + 128]
        return pltpu.make_async_copy(src, (dq_out, dk_out, dv_out)[j], out_sem.at[j])

    def send_grad(j, ref):
        gr[me_p, 0:tok, 128 * j : 128 * j + 128] = summed(ref).astype(bf16)
        each_y(lambda b: g_block(j, me_p, (x, zl, zh, b, c), p_send, b).start())
        g_block(j, me_p, partner, h_send, y).start()
        grad_out(j).start()

    def w_block(j, s, n):
        return send(ws.at[j, s], wr.at[j, n], w_send.at[j, s], w_recv.at[j, n], at_zh(s))

    def send_weight(j):
        def land(b):
            s = b * nc + c
            g_block(j, s, partner, h_send, b).wait_recv()
            g_block(j, s, partner, h_send, b).start()

        each_y(land)

        def land_rest(b, carry):
            g_block(j, b * nc + other, partner, h_send, b).wait_recv()
            return carry

        lax.fori_loop(0, ny, land_rest, 0)
        acc = dot(xr[0], gr[0, :, 128 * j : 128 * j + 128])
        for p in range(1, npc):
            acc = acc + dot(xr[p], gr[p, :, 128 * j : 128 * j + 128])
        for n in range(nzh):
            ws[j, n] = acc[n * chunk : (n + 1) * chunk, :].astype(bf16)
        each(zh, nzh, lambda s: w_block(j, s, zh).start())
        wr[j, zh] = ws[j, zh]

    def a_block(j, s, n):
        return send(ar.at[j, n], ar.at[j, n], a_send.at[j, s], a_recv.at[j, n], at_r(s))

    def send_rows(j):
        each(zh, nzh, lambda s: w_block(j, s, s).wait_recv())
        ar[j, me_r] = summed(wr.at[j]).astype(bf16)
        each(me_r, nr, lambda s: a_block(j, s, me_r).start())

    def weight_out(j):
        lanes = slice(128 * j, 128 * j + 128)
        return pltpu.make_async_copy(wg.at[:, lanes], wg_out.at[:, lanes], out_sem.at[3 + j])

    def finish(j):
        each(me_r, nr, lambda s: a_block(j, s, s).wait_recv())
        wg[:, 128 * j : 128 * j + 128] = summed(ar.at[j])
        weight_out(j).start()

    grad_tiles(1, 0, nx)
    dvr[me_k] = dvs[mine_k, :]
    query_grads()
    lax.fori_loop(0, nz, send_pair, 0)
    grad_tiles(0, 0, 1)
    send_dq()
    grad_tiles(0, 1, nx)
    dkr[me_k] = dks[mine_k, :]
    each(me_k, nk, lambda s: kv_block(1, s, s).wait_recv())
    send_grad(2, dvr)
    own.wait()
    each(me_p, npc, lambda s: x_block(s, s).wait_recv())
    send_weight(2)
    each_z(lambda w: dq_block(w, w).wait_recv())
    send_grad(0, dqr)
    each(me_k, nk, lambda s: kv_block(0, s, s).wait_recv())
    send_grad(1, dkr)
    send_rows(2)
    send_weight(0)
    send_weight(1)
    finish(2)
    send_rows(0)
    send_rows(1)
    finish(0)
    finish(1)

    for m in range(4):
        each_z(lambda w: q_block(m, me_q, partner, q_send, w).wait_send())

        def f_left(w, carry):
            q_block(m, me_q, partner, f_send, w).wait_send()
            return carry

        lax.fori_loop(0, nz, f_left, 0)

    def pair_left(w, carry):
        pair_block(w, other).wait_send()
        return carry

    lax.fori_loop(0, nz, pair_left, 0)
    each_z(lambda w: dq_block(w, z).wait_send())

    def k_left(s):
        for j in range(2):
            k_block(j, me_k, partner, s).wait_send()
            kv_block(j, s, me_k).wait_send()

    each(me_k, nk, k_left)
    each(me_p, npc, lambda s: x_block(s, me_p).wait_send())

    for j in range(3):
        each_y(lambda b: g_block(j, me_p, partner, p_send, b).wait_send())

        def h_left(b, carry):
            g_block(j, me_p, partner, h_send, b).wait_send()
            return carry

        lax.fori_loop(0, ny, h_left, 0)
        each(zh, nzh, lambda s: w_block(j, s, zh).wait_send())
        each(me_r, nr, lambda s: a_block(j, s, me_r).wait_send())
        grad_out(j).wait()
        weight_out(j).wait()


def hand_out(*refs):
    count = len(refs) // 3
    sources, results, held, sems = refs[:count], refs[count : 2 * count], refs[2 * count : -1], refs[-1]
    into = [pltpu.make_async_copy(sources[i], held[i], sems.at[0, i]) for i in range(count)]
    out = [pltpu.make_async_copy(held[i], results[i], sems.at[1, i]) for i in range(count)]
    for copy in into:
        copy.start()
    for i in range(count):
        into[i].wait()
        out[i].start()
    for copy in out:
        copy.wait()


def local(
    dims, layer_input, queries, key_states, value_states, forward_out, out_grad, token_pos,
    block_sample,
):
    nx, nzl, nzh, ny, nc = dims
    tok = queries.shape[0]
    depth = layer_input.shape[1]
    chunk = depth // (nzh * ny * nc)
    nq, nk, npc, nr = nzh * nzl * nc, nx * ny, ny * nc, nx * nzl
    n_query, n_key = nq * tok, nk * tok
    pos = token_pos.reshape(-1, 128)
    nz = nzh * nzl
    V = pltpu.VMEM
    dma = pltpu.SemaphoreType.DMA
    scratch = [
        V((n_query, 128), bf16), V((n_query, 128), bf16), V((tok, 128), bf16), V((nq, 1, 256), f32),
        V((n_key, 128), bf16), V((n_key, 128), bf16), V((tok, depth), bf16),
        V(pos.shape, jnp.int32), pltpu.SMEM(block_sample.shape, jnp.int32), V((256, 128), f32),
        V((n_query, 128), bf16), V((n_key, 128), bf16), V((128, n_key), bf16),
        V((n_key, n_query), bf16), V((n_key, n_query), bf16), V((ny * tok, nzl * nc * tok), f32),
        V((128, n_query), f32), V((nq, 2, n_query), f32),
        V((nx, 1, n_query), f32), V((nx, 1, n_query), f32), V((nx, 1, n_query), f32), V((8, n_query), f32),
        V((n_query, 128), bf16), V((n_query, 128), bf16),
        V((n_query, 128), bf16), V((nz, tok, 128), bf16), V((nz, tok, 128), bf16),
        V((nz, tok, 128), bf16),
        V((n_key, 128), bf16), V((n_key, 128), bf16),
        V((nk, tok, 128), bf16), V((nk, tok, 128), bf16),
        V((npc, nzh * chunk, 256), bf16), V((npc, nzh * chunk, 256), bf16),
        V((npc, 256, 384), bf16), V((3, nzh, chunk, 128), bf16), V((3, nzh, chunk, 128), bf16),
        V((3, nr, chunk, 128), bf16), V((chunk, 384), f32),
        dma((4, nz)), dma((4, nq)), dma((4, nz)),
        dma((nz,)), dma((nz,)), dma((nz,)), dma((nz,)),
        dma((4, nk)), dma((4, nk)), dma((npc,)), dma((npc,)),
        dma((3, ny)), dma((3, ny)), dma((3, npc)),
        dma((3, nzh)), dma((3, nzh)), dma((3, nr)), dma((3, nr)), dma, dma((8,)), dma((6,)),
    ]

    def body(*refs):
        kernel(dims, *refs)

    hbm = pl.BlockSpec(memory_space=pl.ANY)
    grad = jax.ShapeDtypeStruct((tok, 128), bf16)
    shapes = (grad, grad, grad, jax.ShapeDtypeStruct((chunk, 384), f32))
    results = pl.pallas_call(
        body,
        out_shape=shapes,
        in_specs=[hbm] * 8,
        out_specs=(hbm,) * 4,
        scratch_shapes=scratch,
        compiler_params=pltpu.CompilerParams(
            collective_id=0, has_side_effects=True, vmem_limit_bytes=64 * 2**20
        ),
        name="packed_backward",
    )(queries, key_states, value_states, forward_out, out_grad, layer_input, pos, block_sample)
    return pl.pallas_call(
        hand_out,
        out_shape=shapes,
        in_specs=[hbm] * 4,
        out_specs=(hbm,) * 4,
        scratch_shapes=[V(a.shape, a.dtype) for a in shapes] + [dma((2, 4))],
        name="hand_out",
    )(*results)


def on_mesh(finer):
    dims = tuple(finer.shape[a] for a in AXES)
    slots, cols = P(AXES, None), P(("zh", "y", "c"), None)
    return jax.shard_map(
        lambda *args: local(dims, *args),
        mesh=finer,
        in_specs=(slots,) * 6 + (P(), P()),
        out_specs=(slots, slots, slots, cols),
        check_vma=False,
    )


def solution(mesh):
    return on_mesh(Mesh(mesh.devices.reshape(4, 2, 4, 4, 2), AXES))
```

```python
import math

import jax
import jax.numpy as jnp
from jax import lax
from jax.experimental import pallas as pl
from jax.experimental.pallas import tpu as pltpu
from jax.sharding import Mesh
from jax.sharding import PartitionSpec as P

BLK = 128
BIG = 16384.0
MESH = pl.DeviceIdType.MESH
NT = (((1,), (1,)), ((), ()))
AXES = ("x", "zl", "zh", "y", "c")
bf16 = jnp.bfloat16
f32 = jnp.float32


def dot_nt(a, b, **kw):
    return lax.dot_general(a, b, NT, preferred_element_type=f32, **kw)


def dot(a, b):
    return jnp.dot(a, b, preferred_element_type=f32)


def as_column(row):
    return jnp.transpose(jnp.broadcast_to(row, (128, row.shape[1])))


def eye(n):
    return (
        lax.broadcasted_iota(jnp.int32, (n, n), 0) == lax.broadcasted_iota(jnp.int32, (n, n), 1)
    ).astype(bf16)


def by_distance(n):
    return sorted(range(1, n), key=lambda d: -min(d, n - d))


def near(i):
    return i + i // 2 - 2 * (i // 3)


def kernel(
    dims, q_in, k_in, v_in, o_in, g_in, x_in, pos_ref, block_ref,
    dq_out, dk_out, dv_out, wg_out,
    qb, gb, ob, db, kb, vb, xb, pos, blocks, column, fq, fk, kt, et, ut, s_scr, dqt, st, pk, lk, wk, rr,
    gs, qs,
    dqs, dqp, dqc, dqr, dks, dvs, dkr, dvr, xt, xr, gr, ws, wr, ar, wg,
    q_send, q_recv, f_send, e_send, e_recv, d_send, d_recv, k_send, k_recv,
    x_send, x_recv, p_send, h_send, p_recv, w_send, w_recv, a_send, a_recv, own_sem, in_sem, out_sem,
):
    nx, nzl, nzh, ny, nc = dims
    tok = q_in.shape[0]
    chunk = wg_out.shape[0]
    n_block = block_ref.shape[0]
    x, zl, zh, y, c = (lax.axis_index(a) for a in AXES)
    nz = nzh * nzl
    nq, nk, npc, nr = nz * nc, nx * ny, ny * nc, nx * nzl
    z = zh * nzl + zl
    me_q = z * nc + c
    me_k = x * ny + y
    me_p = y * nc + c
    me_r = x * nzl + zl
    n_query, n_key = nq * tok, nk * tok
    key_chunk, query_chunk = ny * tok, nzl * nc * tok

    def rows_of(s):
        return pl.ds(pl.multiple_of(s * tok, tok), tok)

    def at_z(w, core):
        return (x, lax.rem(w, nzl), w // nzl, y, core)

    def at_xy(a, b):
        return (a, zl, zh, b, c)

    def at_p(s):
        return (x, zl, zh, s // nc, lax.rem(s, nc))

    def at_zh(s):
        return (x, zl, s, y, c)

    def at_r(s):
        return (s // nzl, lax.rem(s, nzl), zh, y, c)

    other = 1 - c
    partner = (x, zl, zh, y, other)

    def send(src, dst, send_sem, recv_sem, device):
        return pltpu.make_async_remote_copy(
            src_ref=src, dst_ref=dst, send_sem=send_sem, recv_sem=recv_sem,
            device_id=device, device_id_type=MESH,
        )

    def each(me, size, body):
        def step(i, carry):
            body(lax.rem(me + i, size))
            return carry

        lax.fori_loop(1, size, step, 0)

    def each_z(body):
        for d in by_distance(nz):
            body(lax.rem(z + d, nz))

    def each_y(body):
        for d in by_distance(ny):
            body(lax.rem(y + d, ny))

    def each_xy(body):
        for i in range(nx):
            for n in range(ny):
                if i or n:
                    body(lax.rem(x + nx - near(i), nx), lax.rem(y + ny - near(n), ny))

    def chunk_z(i, body):
        h = lax.rem(zh + near(i), nzh)
        for n in range(nzl):
            w = h * nzl + n
            if i:
                body(w)
            else:
                pl.when(w != z)(lambda w=w: body(w))

    mine_q, mine_k = rows_of(me_q), rows_of(me_k)
    staged = [
        pltpu.make_async_copy(src, dst, in_sem.at[i])
        for i, (src, dst) in enumerate(
            (
                (k_in, kb.at[mine_k, :]), (q_in, qb.at[mine_q, :]), (v_in, vb.at[mine_k, :]),
                (g_in, gb.at[mine_q, :]), (o_in, ob), (pos_ref, pos), (block_ref, blocks), (x_in, xb),
            )
        )
    ]
    for copy in staged:
        copy.start()

    barrier = pltpu.get_barrier_semaphore()

    def hello(device):
        pl.semaphore_signal(barrier, inc=1, device_id=device, device_id_type=MESH)

    each_z(lambda w: hello(at_z(w, c)))
    hello(partner)
    each_xy(lambda a, b: hello(at_xy(a, b)))
    each_y(lambda b: hello((x, zl, zh, b, other)))

    def across(a):
        for n in range(1, nzl):
            hello((a, lax.rem(zl + n, nzl), zh, y, c))

    for n in range(1, nx):
        across(lax.rem(x + n, nx))

    for copy in staged[:5]:
        copy.wait()
    product = gb[mine_q, :].astype(f32) * ob[...].astype(f32)
    delta = dot_nt(jnp.ones((8, product.shape[1]), f32), product, precision=lax.Precision.HIGHEST)
    db[me_q, :, 0:tok] = delta[0:1, :]
    pl.semaphore_wait(barrier, nz + nk + ny - 2 + (nx - 1) * (nzl - 1))

    def q_block(m, s, device, sem, n):
        ref = (qb.at[rows_of(s), :], gb.at[rows_of(s), :], db.at[s], st.at[s])[m]
        return send(ref, ref, sem.at[m, n], q_recv.at[m, s], device)

    def k_block(m, s, device, n):
        ref = (kb, vb)[m].at[rows_of(s), :]
        return send(ref, ref, k_send.at[m, n], k_recv.at[m, s], device)

    def start_q(m):
        for i in range(nzh):
            h = lax.rem(zh + nzh - near(i), nzh)
            for n in range(nzl):
                w = h * nzl + n
                copy = q_block(m, me_q, at_z(w, c), q_send, w)
                if i:
                    copy.start()
                else:
                    pl.when(w != z)(copy.start)
        q_block(m, me_q, partner, f_send, z).start()

    def start_k(m):
        each_xy(lambda a, b: k_block(m, me_k, at_xy(a, b), a * ny + b).start())

    def hand_on(m, i):
        def land(w):
            s = w * nc + c
            q_block(m, s, partner, f_send, w).wait_recv()
            q_block(m, s, partner, f_send, w).start()

        chunk_z(i, land)

    def land_q(m, i):
        h = lax.rem(zh + near(i), nzh)
        for n in range(nzl):
            w = h * nzl + n
            q_block(m, w * nc + other, partner, f_send, w).wait_recv()

    def land_k(m, i):
        a = lax.rem(x + near(i), nx)
        for n in range(ny):
            if i or n:
                s = a * ny + lax.rem(y + near(n), ny)
                k_block(m, s, partner, s).wait_recv()

    start_q(0)
    start_k(0)

    for copy in staged[5:]:
        copy.wait()
    samples = lax.broadcasted_iota(jnp.int32, (1, 128), 1)

    def count(b, carry):
        below, upto = carry
        sample = blocks[b]
        return (
            below + jnp.where(sample < samples, float(BLK), 0.0),
            upto + jnp.where(sample <= samples, float(BLK), 0.0),
        )

    none = jnp.zeros((1, 128), f32)
    low, high = lax.fori_loop(0, n_block, count, (none, none))
    last = lax.broadcasted_iota(jnp.int32, (tok, 128), 1) == 127

    def one_hot(device, hit, always):
        index = device[0]
        for n, i in zip(dims[1:], device[1:]):
            index = index * n + i
        first = index * tok // 128
        skip = pl.multiple_of(lax.rem(index * tok, 128), 32)
        row = jnp.concatenate([pos[pl.ds(first, 1), :], pos[pl.ds(first + 1, 1), :]], axis=1)
        column[...] = as_column(row.astype(f32))
        col = column[pl.ds(skip, tok), :]
        inside = jnp.where((col >= low) & (col < high), hit, 0.0)
        return jnp.where(last, always, inside).astype(bf16)

    def query_hot(s, carry):
        fq[rows_of(s), :] = one_hot(at_z(s // nc, lax.rem(s, nc)), BIG, -BIG)
        return carry

    def key_hot(s, carry):
        fk[rows_of(s), :] = one_hot(at_xy(s // ny, lax.rem(s, ny)), 1.0, 1.0)
        return carry

    lax.fori_loop(0, nk, key_hot, 0)

    lax.fori_loop(0, nq, query_hot, 0)

    xt[:, :, tok:] = jnp.zeros((npc, nzh * chunk, 256 - tok), bf16)
    gr[:, tok:, :] = jnp.zeros((npc, 256 - tok, 384), bf16)
    four = eye(4 * chunk)
    for g in range(nzh * npc // 4):
        turned = dot_nt(four, xb[:, g * 4 * chunk : (g + 1) * 4 * chunk]).astype(bf16)
        for j in range(4):
            n = 4 * g + j
            rows = slice(n // npc * chunk, (n // npc + 1) * chunk)
            xt[n % npc, rows, 0:tok] = turned[j * chunk : (j + 1) * chunk, :]

    def x_block(s, n):
        return send(xt.at[s], xr.at[n], x_send.at[s], x_recv.at[n], at_p(s))

    own = pltpu.make_async_copy(xt.at[me_p], xr.at[me_p], own_sem)
    own.start()

    tq = 256
    score_scale = 1.0 / math.sqrt(128.0)
    rate = score_scale / math.log(2.0)
    def tile(t):
        return pl.ds(pl.multiple_of(t * tq, tq), tq)

    def sweep(moved, block):
        @pl.loop(0, nx * nx)
        def _(t):
            for i in range(nx):

                @pl.when(t == i * i)
                def _():
                    for m in moved:
                        hand_on(m, i)
                    land_k(moved[0], i)

                @pl.when(t == i * i + i)
                def _():
                    for m in moved:
                        land_q(m, i)

            shell = sum(jnp.where(t >= i * i, 1, 0) for i in range(1, nx))
            rest = t - shell * shell
            inner = rest < shell
            ki, qi = jnp.where(inner, shell, rest - shell), jnp.where(inner, rest, shell)
            block(lax.rem(x + near(ki), nx), lax.rem(zh + near(qi), nzh), t)

    def chunk_rows(n, size):
        return pl.ds(pl.multiple_of(n * size, size), size)

    def score_block(kc, qc, t):
        @pl.when(t == min(3, nx * nx - 1))
        def _():
            start_q(2)
            start_q(1)
            start_k(1)

        span, at = chunk_rows(kc, key_chunk), chunk_rows(qc, query_chunk)
        query_tile = jnp.concatenate([qb[at, :], fq[at, :]], axis=1)
        s = dot_nt(jnp.concatenate([kb[span, :], fk[span, :]], axis=1), query_tile)
        s_scr[...] = s
        top = jnp.max(s.reshape(key_chunk // 8, 8, query_chunk), axis=0)
        peak = jnp.max(top, axis=0, keepdims=True)
        e = jnp.exp2((s_scr[...] - peak) * rate)
        total = jnp.sum(e.reshape(key_chunk // 8, 8, query_chunk), axis=0)
        et[span, at] = e.astype(bf16)
        pk[kc, :, at] = peak
        lk[kc, :, at] = jnp.sum(total, axis=0, keepdims=True)

    def grad_block(kc, qc, t):
        span, at = chunk_rows(kc, key_chunk), chunk_rows(qc, query_chunk)
        for i in range(nx):

            @pl.when(t == i * i + i)
            def _():
                rows = [db[qc * nzl * nc + n, :, 0:tok] for n in range(nzl * nc)]
                rr[2:3, at] = jnp.concatenate(rows, axis=1)

        @pl.when(t == nx * nx - 3)
        def _():
            for i in range(nzh):
                hand_on(3, i)

        values = vb[span, :]
        for first in range(0, query_chunk, tq):
            wide = min(tq, query_chunk - first)
            part = pl.ds(pl.multiple_of(qc * query_chunk + first, 128), wide)
            slope = dot_nt(values, gb[part, :]) - rr[2:3, part]
            e = et[span, part].astype(f32) * wk[kc, :, part]
            u = (e * slope).astype(bf16)
            et[span, part] = e.astype(bf16)
            ut[span, part] = u

    sweep((0,), score_block)

    peak = pk[0]
    for n in range(1, nx):
        peak = jnp.maximum(peak, pk[n])
    total = jnp.zeros_like(peak)
    for n in range(nx):
        weight = jnp.exp2((pk[n] - peak) * rate)
        wk[n] = weight
        total = total + lk[n] * weight
    rr[0:1, :] = peak
    rr[1:2, :] = total
    st[me_q] = rr[0:2, :]
    start_q(3)

    def x_block(s, n):
        return send(xt.at[s], xr.at[n], x_send.at[s], x_recv.at[n], at_p(s))

    each(me_p, npc, lambda s: x_block(s, me_p).start())
    kt[...] = dot_nt(eye(128), kb[...]).astype(bf16)
    sweep((1, 2), grad_block)
    wide = 512 if n_query % 512 == 0 else tq

    @pl.loop(0, n_query // wide)
    def _(t):
        at = pl.ds(pl.multiple_of(t * wide, wide), wide)
        dqt[:, at] = dot(kt[...], ut[:, at])

    for i in range(nzh):
        land_q(3, i)

    peak = st[0, 0:1, :]
    for s in range(1, nq):
        peak = jnp.maximum(peak, st[s, 0:1, :])
    total = jnp.zeros_like(peak)
    for s in range(nq):
        total = total + st[s, 1:2, :] * jnp.exp2((st[s, 0:1, :] - peak) * rate)
    rr[3:4, :] = jnp.exp2((rr[0:1, :] - peak) * rate) / total

    def scale_rows(t):
        at = tile(t)
        factor = rr[3:4, at]
        dqs[at, :] = jnp.transpose(dqt[:, at] * (factor * score_scale)).astype(bf16)
        col = as_column(factor)
        gs[at, :] = (gb[at, :].astype(f32) * col).astype(bf16)
        qs[at, :] = (qb[at, :].astype(f32) * (col * score_scale)).astype(bf16)

    pl.loop(0, n_query // tq)(scale_rows)

    def pair_block(w, core):
        src = dqs.at[rows_of(w * nc + core), :]
        return send(src, dqp.at[w], e_send.at[w], e_recv.at[w], partner)

    def dq_block(w, n):
        return send(dqc.at[w], dqr.at[n], d_send.at[w], d_recv.at[n], at_z(w, c))

    def send_pair(w, carry):
        pair_block(w, other).start()
        return carry

    lax.fori_loop(0, nz, send_pair, 0)

    def send_dq():
        def add(w):
            pair_block(w, c).wait_recv()
            mine = dqs[rows_of(w * nc + c), :].astype(f32)
            dqc[w] = (mine + dqp[w].astype(f32)).astype(bf16)

        def step(w):
            add(w)
            dq_block(w, z).start()

        each_z(step)
        add(z)
        dqr[z] = dqc[z]

    tb = ny * tok

    def kv_block(j, s, n):
        src, dst = ((dks, dkr), (dvs, dvr))[j]
        device = at_xy(s // ny, lax.rem(s, ny))
        return send(src.at[rows_of(s), :], dst.at[n], k_send.at[2 + j, s], k_recv.at[2 + j, n], device)

    def grad_tiles(j, first, end):
        out, left, right = ((dks, ut, qs), (dvs, et, gs))[j]

        def step(i, carry):
            t = lax.rem(x + 2 + i, nx)
            at = pl.ds(pl.multiple_of(t * tb, tb), tb)
            out[at, :] = dot(left[at, :], right[...]).astype(bf16)
            for b in range(ny):
                s = t * ny + b

                @pl.when(s != me_k)
                def _():
                    kv_block(j, s, me_k).start()

            return carry

        lax.fori_loop(first, end, step, 0)

    def summed(ref):
        acc = ref[0].astype(f32)
        for s in range(1, ref.shape[0]):
            acc = acc + ref[s].astype(f32)
        return acc

    def g_block(j, s, device, sem, n):
        ref = gr.at[s, 0:tok, 128 * j : 128 * j + 128]
        return send(ref, ref, sem.at[j, n], p_recv.at[j, s], device)

    def grad_out(j):
        src = gr.at[me_p, 0:tok, 128 * j : 128 * j + 128]
        return pltpu.make_async_copy(src, (dq_out, dk_out, dv_out)[j], out_sem.at[j])

    def send_grad(j, ref):
        gr[me_p, 0:tok, 128 * j : 128 * j + 128] = summed(ref).astype(bf16)
        each_y(lambda b: g_block(j, me_p, (x, zl, zh, b, c), p_send, b).start())
        g_block(j, me_p, partner, h_send, y).start()
        grad_out(j).start()

    def w_block(j, s, n):
        return send(ws.at[j, s], wr.at[j, n], w_send.at[j, s], w_recv.at[j, n], at_zh(s))

    def send_weight(j):
        def land(b):
            s = b * nc + c
            g_block(j, s, partner, h_send, b).wait_recv()
            g_block(j, s, partner, h_send, b).start()

        each_y(land)

        def land_rest(b, carry):
            g_block(j, b * nc + other, partner, h_send, b).wait_recv()
            return carry

        lax.fori_loop(0, ny, land_rest, 0)
        acc = dot(xr[0], gr[0, :, 128 * j : 128 * j + 128])
        for p in range(1, npc):
            acc = acc + dot(xr[p], gr[p, :, 128 * j : 128 * j + 128])
        for n in range(nzh):
            ws[j, n] = acc[n * chunk : (n + 1) * chunk, :].astype(bf16)
        each(zh, nzh, lambda s: w_block(j, s, zh).start())
        wr[j, zh] = ws[j, zh]

    def a_block(j, s, n):
        return send(ar.at[j, n], ar.at[j, n], a_send.at[j, s], a_recv.at[j, n], at_r(s))

    def send_rows(j):
        each(zh, nzh, lambda s: w_block(j, s, s).wait_recv())
        ar[j, me_r] = summed(wr.at[j]).astype(bf16)
        each(me_r, nr, lambda s: a_block(j, s, me_r).start())

    def weight_out(j):
        lanes = slice(128 * j, 128 * j + 128)
        return pltpu.make_async_copy(wg.at[:, lanes], wg_out.at[:, lanes], out_sem.at[3 + j])

    def finish(j):
        each(me_r, nr, lambda s: a_block(j, s, s).wait_recv())
        wg[:, 128 * j : 128 * j + 128] = summed(ar.at[j])
        weight_out(j).start()

    grad_tiles(1, 0, 1)
    send_dq()
    grad_tiles(1, 1, nx)
    dvr[me_k] = dvs[mine_k, :]
    grad_tiles(0, 0, nx)
    dkr[me_k] = dks[mine_k, :]
    for m in range(4):
        each_z(lambda w: q_block(m, me_q, partner, q_send, w).wait_send())

        def f_left(w, carry):
            q_block(m, me_q, partner, f_send, w).wait_send()
            return carry

        lax.fori_loop(0, nz, f_left, 0)

    for j in range(2):
        each(me_k, nk, lambda s: k_block(j, me_k, partner, s).wait_send())

    each_z(lambda w: dq_block(w, w).wait_recv())
    send_grad(0, dqr)
    own.wait()
    each(me_p, npc, lambda s: x_block(s, s).wait_recv())
    each(me_k, nk, lambda s: kv_block(1, s, s).wait_recv())
    send_grad(2, dvr)
    send_weight(0)
    each(me_k, nk, lambda s: kv_block(0, s, s).wait_recv())
    send_grad(1, dkr)
    send_weight(2)
    send_rows(0)
    send_weight(1)
    send_rows(2)
    finish(0)
    send_rows(1)

    def pair_left(w, carry):
        pair_block(w, other).wait_send()
        return carry

    lax.fori_loop(0, nz, pair_left, 0)
    each_z(lambda w: dq_block(w, z).wait_send())

    def k_left(s):
        for j in range(2):
            kv_block(j, s, me_k).wait_send()

    each(me_k, nk, k_left)
    each(me_p, npc, lambda s: x_block(s, me_p).wait_send())

    for j in range(3):
        each_y(lambda b: g_block(j, me_p, partner, p_send, b).wait_send())

        def h_left(b, carry):
            g_block(j, me_p, partner, h_send, b).wait_send()
            return carry

        lax.fori_loop(0, ny, h_left, 0)
        each(zh, nzh, lambda s: w_block(j, s, zh).wait_send())
        grad_out(j).wait()

    finish(2)
    finish(1)
    for j in range(3):
        each(me_r, nr, lambda s: a_block(j, s, me_r).wait_send())
        weight_out(j).wait()


def hand_out(*refs):
    count = len(refs) // 3
    sources, results, held, sems = refs[:count], refs[count : 2 * count], refs[2 * count : -1], refs[-1]
    into = [pltpu.make_async_copy(sources[i], held[i], sems.at[0, i]) for i in range(count)]
    out = [pltpu.make_async_copy(held[i], results[i], sems.at[1, i]) for i in range(count)]
    for copy in into:
        copy.start()
    for i in range(count):
        into[i].wait()
        out[i].start()
    for copy in out:
        copy.wait()


def local(
    dims, layer_input, queries, key_states, value_states, forward_out, out_grad, token_pos,
    block_sample,
):
    nx, nzl, nzh, ny, nc = dims
    tok = queries.shape[0]
    depth = layer_input.shape[1]
    chunk = depth // (nzh * ny * nc)
    nq, nk, npc, nr = nzh * nzl * nc, nx * ny, ny * nc, nx * nzl
    n_query, n_key = nq * tok, nk * tok
    pos = token_pos.reshape(-1, 128)
    nz = nzh * nzl
    V = pltpu.VMEM
    dma = pltpu.SemaphoreType.DMA
    scratch = [
        V((n_query, 128), bf16), V((n_query, 128), bf16), V((tok, 128), bf16), V((nq, 1, 256), f32),
        V((n_key, 128), bf16), V((n_key, 128), bf16), V((tok, depth), bf16),
        V(pos.shape, jnp.int32), pltpu.SMEM(block_sample.shape, jnp.int32), V((256, 128), f32),
        V((n_query, 128), bf16), V((n_key, 128), bf16), V((128, n_key), bf16),
        V((n_key, n_query), bf16), V((n_key, n_query), bf16), V((ny * tok, nzl * nc * tok), f32),
        V((128, n_query), f32), V((nq, 2, n_query), f32),
        V((nx, 1, n_query), f32), V((nx, 1, n_query), f32), V((nx, 1, n_query), f32), V((8, n_query), f32),
        V((n_query, 128), bf16), V((n_query, 128), bf16),
        V((n_query, 128), bf16), V((nz, tok, 128), bf16), V((nz, tok, 128), bf16),
        V((nz, tok, 128), bf16),
        V((n_key, 128), bf16), V((n_key, 128), bf16),
        V((nk, tok, 128), bf16), V((nk, tok, 128), bf16),
        V((npc, nzh * chunk, 256), bf16), V((npc, nzh * chunk, 256), bf16),
        V((npc, 256, 384), bf16), V((3, nzh, chunk, 128), bf16), V((3, nzh, chunk, 128), bf16),
        V((3, nr, chunk, 128), bf16), V((chunk, 384), f32),
        dma((4, nz)), dma((4, nq)), dma((4, nz)),
        dma((nz,)), dma((nz,)), dma((nz,)), dma((nz,)),
        dma((4, nk)), dma((4, nk)), dma((npc,)), dma((npc,)),
        dma((3, ny)), dma((3, ny)), dma((3, npc)),
        dma((3, nzh)), dma((3, nzh)), dma((3, nr)), dma((3, nr)), dma, dma((8,)), dma((6,)),
    ]

    def body(*refs):
        kernel(dims, *refs)

    hbm = pl.BlockSpec(memory_space=pl.ANY)
    grad = jax.ShapeDtypeStruct((tok, 128), bf16)
    shapes = (grad, grad, grad, jax.ShapeDtypeStruct((chunk, 384), f32))
    results = pl.pallas_call(
        body,
        out_shape=shapes,
        in_specs=[hbm] * 8,
        out_specs=(hbm,) * 4,
        scratch_shapes=scratch,
        compiler_params=pltpu.CompilerParams(
            collective_id=0, has_side_effects=True, vmem_limit_bytes=64 * 2**20
        ),
        name="packed_backward",
    )(queries, key_states, value_states, forward_out, out_grad, layer_input, pos, block_sample)
    return pl.pallas_call(
        hand_out,
        out_shape=shapes,
        in_specs=[hbm] * 4,
        out_specs=(hbm,) * 4,
        scratch_shapes=[V(a.shape, a.dtype) for a in shapes] + [dma((2, 4))],
        name="hand_out",
    )(*results)


def on_mesh(finer):
    dims = tuple(finer.shape[a] for a in AXES)
    slots, cols = P(AXES, None), P(("zh", "y", "c"), None)
    return jax.shard_map(
        lambda *args: local(dims, *args),
        mesh=finer,
        in_specs=(slots,) * 6 + (P(), P()),
        out_specs=(slots, slots, slots, cols),
        check_vma=False,
    )


def solution(mesh):
    return on_mesh(Mesh(mesh.devices.reshape(4, 2, 4, 4, 2), AXES))
```

```python
import math

import jax
import jax.numpy as jnp
from jax import lax
from jax.experimental import pallas as pl
from jax.experimental.pallas import tpu as pltpu
from jax.sharding import Mesh
from jax.sharding import PartitionSpec as P

BLK = 128
BIG = 16384.0
MESH = pl.DeviceIdType.MESH
NT = (((1,), (1,)), ((), ()))
AXES = ("x", "zl", "zh", "y", "c")
bf16 = jnp.bfloat16
f32 = jnp.float32


def dot_nt(a, b, **kw):
    return lax.dot_general(a, b, NT, preferred_element_type=f32, **kw)


def dot(a, b):
    return jnp.dot(a, b, preferred_element_type=f32)


def as_column(row):
    return jnp.transpose(jnp.broadcast_to(row, (128, row.shape[1])))


def eye(n):
    return (
        lax.broadcasted_iota(jnp.int32, (n, n), 0) == lax.broadcasted_iota(jnp.int32, (n, n), 1)
    ).astype(bf16)


def by_distance(n):
    return sorted(range(1, n), key=lambda d: -min(d, n - d))


def near(i):
    return i + i // 2 - 2 * (i // 3)


def kernel(
    dims, q_in, k_in, v_in, o_in, g_in, x_in, pos_ref, block_ref,
    dq_out, dk_out, dv_out, wg_out,
    qb, gb, ob, db, kb, vb, xb, pos, blocks, column, fq, fk, kt, et, ut, s_scr, dqt, st, pk, lk, wk, rr,
    gs, qs,
    dqs, dqp, dqc, dqr, dks, dvs, dkr, dvr, xt, xr, gr, ws, wr, ar, wg,
    q_send, q_recv, f_send, e_send, e_recv, d_send, d_recv, k_send, k_recv,
    x_send, x_recv, p_send, h_send, p_recv, w_send, w_recv, a_send, a_recv, own_sem, in_sem, out_sem,
):
    nx, nzl, nzh, ny, nc = dims
    tok = q_in.shape[0]
    chunk = wg_out.shape[0]
    n_block = block_ref.shape[0]
    x, zl, zh, y, c = (lax.axis_index(a) for a in AXES)
    nz = nzh * nzl
    nq, nk, npc, nr = nz * nc, nx * ny, ny * nc, nx * nzl
    z = zh * nzl + zl
    me_q = z * nc + c
    me_k = x * ny + y
    me_p = y * nc + c
    me_r = x * nzl + zl
    n_query, n_key = nq * tok, nk * tok
    key_chunk, query_chunk = ny * tok, nzl * nc * tok

    def rows_of(s):
        return pl.ds(pl.multiple_of(s * tok, tok), tok)

    def at_z(w, core):
        return (x, lax.rem(w, nzl), w // nzl, y, core)

    def at_xy(a, b):
        return (a, zl, zh, b, c)

    def at_p(s):
        return (x, zl, zh, s // nc, lax.rem(s, nc))

    def at_zh(s):
        return (x, zl, s, y, c)

    def at_r(s):
        return (s // nzl, lax.rem(s, nzl), zh, y, c)

    other = 1 - c
    partner = (x, zl, zh, y, other)

    def send(src, dst, send_sem, recv_sem, device):
        return pltpu.make_async_remote_copy(
            src_ref=src, dst_ref=dst, send_sem=send_sem, recv_sem=recv_sem,
            device_id=device, device_id_type=MESH,
        )

    def each(me, size, body):
        def step(i, carry):
            body(lax.rem(me + i, size))
            return carry

        lax.fori_loop(1, size, step, 0)

    def each_z(body):
        for d in by_distance(nz):
            body(lax.rem(z + d, nz))

    def each_y(body):
        for d in by_distance(ny):
            body(lax.rem(y + d, ny))

    def each_xy(body):
        for i in range(nx):
            for n in range(ny):
                if i or n:
                    body(lax.rem(x + nx - near(i), nx), lax.rem(y + ny - near(n), ny))

    def chunk_z(i, body):
        h = lax.rem(zh + near(i), nzh)
        for n in range(nzl):
            w = h * nzl + n
            if i:
                body(w)
            else:
                pl.when(w != z)(lambda w=w: body(w))

    mine_q, mine_k = rows_of(me_q), rows_of(me_k)
    staged = [
        pltpu.make_async_copy(src, dst, in_sem.at[i])
        for i, (src, dst) in enumerate(
            (
                (k_in, kb.at[mine_k, :]), (q_in, qb.at[mine_q, :]), (v_in, vb.at[mine_k, :]),
                (g_in, gb.at[mine_q, :]), (o_in, ob), (pos_ref, pos), (block_ref, blocks), (x_in, xb),
            )
        )
    ]
    for copy in staged:
        copy.start()

    barrier = pltpu.get_barrier_semaphore()

    def hello(device):
        pl.semaphore_signal(barrier, inc=1, device_id=device, device_id_type=MESH)

    each_z(lambda w: hello(at_z(w, c)))
    hello(partner)
    each_xy(lambda a, b: hello(at_xy(a, b)))
    each_y(lambda b: hello((x, zl, zh, b, other)))

    def across(a):
        for n in range(1, nzl):
            hello((a, lax.rem(zl + n, nzl), zh, y, c))

    for n in range(1, nx):
        across(lax.rem(x + n, nx))

    for copy in staged[:5]:
        copy.wait()
    product = gb[mine_q, :].astype(f32) * ob[...].astype(f32)
    delta = dot_nt(jnp.ones((8, product.shape[1]), f32), product, precision=lax.Precision.HIGHEST)
    db[me_q, :, 0:tok] = delta[0:1, :]
    pl.semaphore_wait(barrier, nz + nk + ny - 2 + (nx - 1) * (nzl - 1))

    def q_block(m, s, device, sem, n):
        ref = (qb.at[rows_of(s), :], gb.at[rows_of(s), :], db.at[s], st.at[s])[m]
        return send(ref, ref, sem.at[m, n], q_recv.at[m, s], device)

    def k_block(m, s, device, n):
        ref = (kb, vb)[m].at[rows_of(s), :]
        return send(ref, ref, k_send.at[m, n], k_recv.at[m, s], device)

    def start_q(m):
        for i in range(nzh):
            h = lax.rem(zh + nzh - near(i), nzh)
            for n in range(nzl):
                w = h * nzl + n
                copy = q_block(m, me_q, at_z(w, c), q_send, w)
                if i:
                    copy.start()
                else:
                    pl.when(w != z)(copy.start)
        q_block(m, me_q, partner, f_send, z).start()

    def start_k(m):
        each_xy(lambda a, b: k_block(m, me_k, at_xy(a, b), a * ny + b).start())

    def hand_on(m, i):
        def land(w):
            s = w * nc + c
            q_block(m, s, partner, f_send, w).wait_recv()
            q_block(m, s, partner, f_send, w).start()

        chunk_z(i, land)

    def land_q(m, i):
        h = lax.rem(zh + near(i), nzh)
        for n in range(nzl):
            w = h * nzl + n
            q_block(m, w * nc + other, partner, f_send, w).wait_recv()

    def land_k(m, i):
        a = lax.rem(x + near(i), nx)
        for n in range(ny):
            if i or n:
                s = a * ny + lax.rem(y + near(n), ny)
                k_block(m, s, partner, s).wait_recv()

    start_q(0)
    start_k(0)

    for copy in staged[5:]:
        copy.wait()
    samples = lax.broadcasted_iota(jnp.int32, (1, 128), 1)

    def count(b, carry):
        below, upto = carry
        sample = blocks[b]
        return (
            below + jnp.where(sample < samples, float(BLK), 0.0),
            upto + jnp.where(sample <= samples, float(BLK), 0.0),
        )

    none = jnp.zeros((1, 128), f32)
    low, high = lax.fori_loop(0, n_block, count, (none, none))
    last = lax.broadcasted_iota(jnp.int32, (tok, 128), 1) == 127

    def one_hot(device, hit, always):
        index = device[0]
        for n, i in zip(dims[1:], device[1:]):
            index = index * n + i
        first = index * tok // 128
        skip = pl.multiple_of(lax.rem(index * tok, 128), 32)
        row = jnp.concatenate([pos[pl.ds(first, 1), :], pos[pl.ds(first + 1, 1), :]], axis=1)
        column[...] = as_column(row.astype(f32))
        col = column[pl.ds(skip, tok), :]
        inside = jnp.where((col >= low) & (col < high), hit, 0.0)
        return jnp.where(last, always, inside).astype(bf16)

    def query_hot(s, carry):
        fq[rows_of(s), :] = one_hot(at_z(s // nc, lax.rem(s, nc)), BIG, -BIG)
        return carry

    def key_hot(s, carry):
        fk[rows_of(s), :] = one_hot(at_xy(s // ny, lax.rem(s, ny)), 1.0, 1.0)
        return carry

    lax.fori_loop(0, nk, key_hot, 0)

    lax.fori_loop(0, nq, query_hot, 0)

    xt[:, :, tok:] = jnp.zeros((npc, nzh * chunk, 256 - tok), bf16)
    gr[:, tok:, :] = jnp.zeros((npc, 256 - tok, 384), bf16)
    four = eye(4 * chunk)
    for g in range(nzh * npc // 4):
        turned = dot_nt(four, xb[:, g * 4 * chunk : (g + 1) * 4 * chunk]).astype(bf16)
        for j in range(4):
            n = 4 * g + j
            rows = slice(n // npc * chunk, (n // npc + 1) * chunk)
            xt[n % npc, rows, 0:tok] = turned[j * chunk : (j + 1) * chunk, :]

    def x_block(s, n):
        return send(xt.at[s], xr.at[n], x_send.at[s], x_recv.at[n], at_p(s))

    own = pltpu.make_async_copy(xt.at[me_p], xr.at[me_p], own_sem)
    own.start()

    tq = 256
    score_scale = 1.0 / math.sqrt(128.0)
    rate = score_scale / math.log(2.0)
    def tile(t):
        return pl.ds(pl.multiple_of(t * tq, tq), tq)

    def sweep(moved, block):
        @pl.loop(0, nx * nx)
        def _(t):
            for i in range(nx):

                @pl.when(t == i * i)
                def _():
                    for m in moved:
                        hand_on(m, i)
                    land_k(moved[0], i)

                @pl.when(t == i * i + i)
                def _():
                    for m in moved:
                        land_q(m, i)

            shell = sum(jnp.where(t >= i * i, 1, 0) for i in range(1, nx))
            rest = t - shell * shell
            inner = rest < shell
            ki, qi = jnp.where(inner, shell, rest - shell), jnp.where(inner, rest, shell)
            block(lax.rem(x + near(ki), nx), lax.rem(zh + near(qi), nzh), t)

    def chunk_rows(n, size):
        return pl.ds(pl.multiple_of(n * size, size), size)

    def score_block(kc, qc, t):
        @pl.when(t == min(3, nx * nx - 1))
        def _():
            start_q(2)
            start_q(1)
            start_k(1)

        span, at = chunk_rows(kc, key_chunk), chunk_rows(qc, query_chunk)
        query_tile = jnp.concatenate([qb[at, :], fq[at, :]], axis=1)
        s = dot_nt(jnp.concatenate([kb[span, :], fk[span, :]], axis=1), query_tile)
        s_scr[...] = s
        top = jnp.max(s.reshape(key_chunk // 8, 8, query_chunk), axis=0)
        peak = jnp.max(top, axis=0, keepdims=True)
        e = jnp.exp2((s_scr[...] - peak) * rate)
        total = jnp.sum(e.reshape(key_chunk // 8, 8, query_chunk), axis=0)
        et[span, at] = e.astype(bf16)
        pk[kc, :, at] = peak
        lk[kc, :, at] = jnp.sum(total, axis=0, keepdims=True)

    def grad_block(kc, qc, t):
        span, at = chunk_rows(kc, key_chunk), chunk_rows(qc, query_chunk)
        for i in range(nx):

            @pl.when(t == i * i + i)
            def _():
                rows = [db[qc * nzl * nc + n, :, 0:tok] for n in range(nzl * nc)]
                rr[2:3, at] = jnp.concatenate(rows, axis=1)

        @pl.when(t == nx * nx - 3)
        def _():
            for i in range(nzh):
                hand_on(3, i)

        values = vb[span, :]
        for first in range(0, query_chunk, tq):
            wide = min(tq, query_chunk - first)
            part = pl.ds(pl.multiple_of(qc * query_chunk + first, 128), wide)
            slope = dot_nt(values, gb[part, :]) - rr[2:3, part]
            e = et[span, part].astype(f32) * wk[kc, :, part]
            u = (e * slope).astype(bf16)
            et[span, part] = e.astype(bf16)
            ut[span, part] = u

    sweep((0,), score_block)

    peak = pk[0]
    for n in range(1, nx):
        peak = jnp.maximum(peak, pk[n])
    total = jnp.zeros_like(peak)
    for n in range(nx):
        weight = jnp.exp2((pk[n] - peak) * rate)
        wk[n] = weight
        total = total + lk[n] * weight
    rr[0:1, :] = peak
    rr[1:2, :] = total
    st[me_q] = rr[0:2, :]
    start_q(3)

    def x_block(s, n):
        return send(xt.at[s], xr.at[n], x_send.at[s], x_recv.at[n], at_p(s))

    each(me_p, npc, lambda s: x_block(s, me_p).start())
    kt[...] = dot_nt(eye(128), kb[...]).astype(bf16)
    sweep((1, 2), grad_block)
    wide = 512 if n_query % 512 == 0 else tq

    @pl.loop(0, n_query // wide)
    def _(t):
        at = pl.ds(pl.multiple_of(t * wide, wide), wide)
        dqt[:, at] = dot(kt[...], ut[:, at])

    for i in range(nzh):
        land_q(3, i)

    peak = st[0, 0:1, :]
    for s in range(1, nq):
        peak = jnp.maximum(peak, st[s, 0:1, :])
    total = jnp.zeros_like(peak)
    for s in range(nq):
        total = total + st[s, 1:2, :] * jnp.exp2((st[s, 0:1, :] - peak) * rate)
    rr[3:4, :] = jnp.exp2((rr[0:1, :] - peak) * rate) / total

    def scale_rows(t):
        at = tile(t)
        factor = rr[3:4, at]
        dqs[at, :] = jnp.transpose(dqt[:, at] * (factor * score_scale)).astype(bf16)
        col = as_column(factor)
        gs[at, :] = (gb[at, :].astype(f32) * col).astype(bf16)
        qs[at, :] = (qb[at, :].astype(f32) * (col * score_scale)).astype(bf16)

    pl.loop(0, n_query // tq)(scale_rows)

    def pair_block(w, core):
        src = dqs.at[rows_of(w * nc + core), :]
        return send(src, dqp.at[w], e_send.at[w], e_recv.at[w], partner)

    def dq_block(w, n):
        return send(dqc.at[w], dqr.at[n], d_send.at[w], d_recv.at[n], at_z(w, c))

    def send_pair(w, carry):
        pair_block(w, other).start()
        return carry

    lax.fori_loop(0, nz, send_pair, 0)

    def send_dq():
        def add(w):
            pair_block(w, c).wait_recv()
            mine = dqs[rows_of(w * nc + c), :].astype(f32)
            dqc[w] = (mine + dqp[w].astype(f32)).astype(bf16)

        def step(w):
            add(w)
            dq_block(w, z).start()

        each_z(step)
        add(z)
        dqr[z] = dqc[z]

    tb = ny * tok

    def kv_block(j, s, n):
        src, dst = ((dks, dkr), (dvs, dvr))[j]
        device = at_xy(s // ny, lax.rem(s, ny))
        return send(src.at[rows_of(s), :], dst.at[n], k_send.at[2 + j, s], k_recv.at[2 + j, n], device)

    def grad_tiles(j, first, end):
        out, left, right = ((dks, ut, qs), (dvs, et, gs))[j]

        def step(i, carry):
            t = lax.rem(x + 2 + i, nx)
            at = pl.ds(pl.multiple_of(t * tb, tb), tb)
            out[at, :] = dot(left[at, :], right[...]).astype(bf16)
            for b in range(ny):
                s = t * ny + b

                @pl.when(s != me_k)
                def _():
                    kv_block(j, s, me_k).start()

            return carry

        lax.fori_loop(first, end, step, 0)

    def summed(ref):
        acc = ref[0].astype(f32)
        for s in range(1, ref.shape[0]):
            acc = acc + ref[s].astype(f32)
        return acc

    def g_block(j, s, device, sem, n):
        ref = gr.at[s, 0:tok, 128 * j : 128 * j + 128]
        return send(ref, ref, sem.at[j, n], p_recv.at[j, s], device)

    def grad_out(j):
        src = gr.at[me_p, 0:tok, 128 * j : 128 * j + 128]
        return pltpu.make_async_copy(src, (dq_out, dk_out, dv_out)[j], out_sem.at[j])

    def send_grad(j, ref):
        gr[me_p, 0:tok, 128 * j : 128 * j + 128] = summed(ref).astype(bf16)
        each_y(lambda b: g_block(j, me_p, (x, zl, zh, b, c), p_send, b).start())
        g_block(j, me_p, partner, h_send, y).start()
        grad_out(j).start()

    def w_block(j, s, n):
        return send(ws.at[j, s], wr.at[j, n], w_send.at[j, s], w_recv.at[j, n], at_zh(s))

    def send_weight(j):
        def land(b):
            s = b * nc + c
            g_block(j, s, partner, h_send, b).wait_recv()
            g_block(j, s, partner, h_send, b).start()

        each_y(land)

        def land_rest(b, carry):
            g_block(j, b * nc + other, partner, h_send, b).wait_recv()
            return carry

        def terms(core):
            parts = [b * nc + core for b in range(ny)]
            return sum(dot(xr[p], gr[p, :, 128 * j : 128 * j + 128]) for p in parts)

        acc = terms(c)
        lax.fori_loop(0, ny, land_rest, 0)
        acc = acc + terms(other)
        for n in range(nzh):
            ws[j, n] = acc[n * chunk : (n + 1) * chunk, :].astype(bf16)
        each(zh, nzh, lambda s: w_block(j, s, zh).start())
        wr[j, zh] = ws[j, zh]

    def a_block(j, s, n):
        return send(ar.at[j, n], ar.at[j, n], a_send.at[j, s], a_recv.at[j, n], at_r(s))

    def send_rows(j):
        each(zh, nzh, lambda s: w_block(j, s, s).wait_recv())
        ar[j, me_r] = summed(wr.at[j]).astype(bf16)
        each(me_r, nr, lambda s: a_block(j, s, me_r).start())

    def weight_out(j):
        lanes = slice(128 * j, 128 * j + 128)
        return pltpu.make_async_copy(wg.at[:, lanes], wg_out.at[:, lanes], out_sem.at[3 + j])

    def finish(j):
        each(me_r, nr, lambda s: a_block(j, s, s).wait_recv())
        wg[:, 128 * j : 128 * j + 128] = summed(ar.at[j])
        weight_out(j).start()

    grad_tiles(1, 0, 1)
    send_dq()
    grad_tiles(1, 1, nx)
    dvr[me_k] = dvs[mine_k, :]
    grad_tiles(0, 0, nx)
    dkr[me_k] = dks[mine_k, :]
    for m in range(4):
        each_z(lambda w: q_block(m, me_q, partner, q_send, w).wait_send())

        def f_left(w, carry):
            q_block(m, me_q, partner, f_send, w).wait_send()
            return carry

        lax.fori_loop(0, nz, f_left, 0)

    for j in range(2):
        each(me_k, nk, lambda s: k_block(j, me_k, partner, s).wait_send())

    each_z(lambda w: dq_block(w, w).wait_recv())
    send_grad(0, dqr)
    own.wait()
    each(me_p, npc, lambda s: x_block(s, s).wait_recv())
    each(me_k, nk, lambda s: kv_block(1, s, s).wait_recv())
    send_grad(2, dvr)
    send_weight(0)
    each(me_k, nk, lambda s: kv_block(0, s, s).wait_recv())
    send_grad(1, dkr)
    send_weight(2)
    send_rows(0)
    send_weight(1)
    send_rows(2)
    finish(0)
    send_rows(1)

    def pair_left(w, carry):
        pair_block(w, other).wait_send()
        return carry

    lax.fori_loop(0, nz, pair_left, 0)
    each_z(lambda w: dq_block(w, z).wait_send())

    def k_left(s):
        for j in range(2):
            kv_block(j, s, me_k).wait_send()

    each(me_k, nk, k_left)
    each(me_p, npc, lambda s: x_block(s, me_p).wait_send())

    for j in range(3):
        each_y(lambda b: g_block(j, me_p, partner, p_send, b).wait_send())

        def h_left(b, carry):
            g_block(j, me_p, partner, h_send, b).wait_send()
            return carry

        lax.fori_loop(0, ny, h_left, 0)
        each(zh, nzh, lambda s: w_block(j, s, zh).wait_send())
        grad_out(j).wait()

    finish(2)
    finish(1)
    for j in range(3):
        each(me_r, nr, lambda s: a_block(j, s, me_r).wait_send())
        weight_out(j).wait()


def hand_out(*refs):
    count = len(refs) // 3
    sources, results, held, sems = refs[:count], refs[count : 2 * count], refs[2 * count : -1], refs[-1]
    into = [pltpu.make_async_copy(sources[i], held[i], sems.at[0, i]) for i in range(count)]
    out = [pltpu.make_async_copy(held[i], results[i], sems.at[1, i]) for i in range(count)]
    for copy in into:
        copy.start()
    for i in range(count):
        into[i].wait()
        out[i].start()
    for copy in out:
        copy.wait()


def local(
    dims, layer_input, queries, key_states, value_states, forward_out, out_grad, token_pos,
    block_sample,
):
    nx, nzl, nzh, ny, nc = dims
    tok = queries.shape[0]
    depth = layer_input.shape[1]
    chunk = depth // (nzh * ny * nc)
    nq, nk, npc, nr = nzh * nzl * nc, nx * ny, ny * nc, nx * nzl
    n_query, n_key = nq * tok, nk * tok
    pos = token_pos.reshape(-1, 128)
    nz = nzh * nzl
    V = pltpu.VMEM
    dma = pltpu.SemaphoreType.DMA
    scratch = [
        V((n_query, 128), bf16), V((n_query, 128), bf16), V((tok, 128), bf16), V((nq, 1, 256), f32),
        V((n_key, 128), bf16), V((n_key, 128), bf16), V((tok, depth), bf16),
        V(pos.shape, jnp.int32), pltpu.SMEM(block_sample.shape, jnp.int32), V((256, 128), f32),
        V((n_query, 128), bf16), V((n_key, 128), bf16), V((128, n_key), bf16),
        V((n_key, n_query), bf16), V((n_key, n_query), bf16), V((ny * tok, nzl * nc * tok), f32),
        V((128, n_query), f32), V((nq, 2, n_query), f32),
        V((nx, 1, n_query), f32), V((nx, 1, n_query), f32), V((nx, 1, n_query), f32), V((8, n_query), f32),
        V((n_query, 128), bf16), V((n_query, 128), bf16),
        V((n_query, 128), bf16), V((nz, tok, 128), bf16), V((nz, tok, 128), bf16),
        V((nz, tok, 128), bf16),
        V((n_key, 128), bf16), V((n_key, 128), bf16),
        V((nk, tok, 128), bf16), V((nk, tok, 128), bf16),
        V((npc, nzh * chunk, 256), bf16), V((npc, nzh * chunk, 256), bf16),
        V((npc, 256, 384), bf16), V((3, nzh, chunk, 128), bf16), V((3, nzh, chunk, 128), bf16),
        V((3, nr, chunk, 128), bf16), V((chunk, 384), f32),
        dma((4, nz)), dma((4, nq)), dma((4, nz)),
        dma((nz,)), dma((nz,)), dma((nz,)), dma((nz,)),
        dma((4, nk)), dma((4, nk)), dma((npc,)), dma((npc,)),
        dma((3, ny)), dma((3, ny)), dma((3, npc)),
        dma((3, nzh)), dma((3, nzh)), dma((3, nr)), dma((3, nr)), dma, dma((8,)), dma((6,)),
    ]

    def body(*refs):
        kernel(dims, *refs)

    hbm = pl.BlockSpec(memory_space=pl.ANY)
    grad = jax.ShapeDtypeStruct((tok, 128), bf16)
    shapes = (grad, grad, grad, jax.ShapeDtypeStruct((chunk, 384), f32))
    results = pl.pallas_call(
        body,
        out_shape=shapes,
        in_specs=[hbm] * 8,
        out_specs=(hbm,) * 4,
        scratch_shapes=scratch,
        compiler_params=pltpu.CompilerParams(
            collective_id=0, has_side_effects=True, vmem_limit_bytes=64 * 2**20
        ),
        name="packed_backward",
    )(queries, key_states, value_states, forward_out, out_grad, layer_input, pos, block_sample)
    return pl.pallas_call(
        hand_out,
        out_shape=shapes,
        in_specs=[hbm] * 4,
        out_specs=(hbm,) * 4,
        scratch_shapes=[V(a.shape, a.dtype) for a in shapes] + [dma((2, 4))],
        name="hand_out",
    )(*results)


def on_mesh(finer):
    dims = tuple(finer.shape[a] for a in AXES)
    slots, cols = P(AXES, None), P(("zh", "y", "c"), None)
    return jax.shard_map(
        lambda *args: local(dims, *args),
        mesh=finer,
        in_specs=(slots,) * 6 + (P(), P()),
        out_specs=(slots, slots, slots, cols),
        check_vma=False,
    )


def solution(mesh):
    return on_mesh(Mesh(mesh.devices.reshape(4, 2, 4, 4, 2), AXES))
```
